512 devices in a mesh: shot: 128 (over z, y, core), tm: 4 (over x).
Axes of the slice: x: 4, y: 8, z: 8, core: 2. Of those that a mesh axis runs over, the one named last changes fastest.
Arguments:
- records: bfloat16 [128, 4, 256, 512], P('shot', None, None, 'tm'), may hold values from -6 to 6
- fan_taps: bfloat16 [4, 15, 15], replicated, may hold values from -0.29882812 to 0.29882812
- dip_taps: bfloat16 [15, 15], replicated, may hold values from -0.29882812 to 0.29882812
- live_mask: int32 [128, 256], P('shot'), may hold values from 0 to 1, as said below
- node_place: int32 [256], replicated, may hold values from 0 to 255, as said below
- shot_place: int32 [128], replicated, may hold values from 0 to 127, as said below
Outputs:
- node_gathers: bfloat16 [128, 4, 256, 512], P(None, None, 'shot', 'tm')
The draws below stay inside these ranges and needn't reach their ends.
Inputs may be any that keep to these rules, and one draw needn't show every extreme that they name: `live_mask`: A trace is live only where the node lies within 128 positions of the shot's point on the receiver line; some traces inside that band are dead too. `node_place`: A permutation: every position once. `shot_place`: A permutation: every position once.
All inputs are finite; a program needn't handle non-finite values.
Results may differ from the reference program's by a relative error of at most 0.0049.
Values may be sent and summed in bfloat16 or wider, within the bound.
No kernel may reach another device: no remote copies, remote signals or barrier semaphores. Data moves between devices by JAX's collectives and lax.ppermute only.
A program may use at most 64 MiB of HBM per device.

```python
import jax
import jax.numpy as jnp
from jax import lax

C = 4
TAPS = 15
SHOTS = 128
NODES = 256
TIME = 512


def geometry(key):
    node_place = jax.random.permutation(jax.random.fold_in(key, 101), NODES).astype(jnp.int32)
    shot_place = jax.random.permutation(jax.random.fold_in(key, 102), SHOTS).astype(jnp.int32)
    source_spot = shot_place * NODES // SHOTS
    offset = jnp.abs(source_spot[:, None] - node_place[None, :])
    recorded = jax.random.randint(jax.random.fold_in(key, 103), (SHOTS, NODES), 0, 16)
    live_mask = jnp.where((offset <= NODES // 2) & (recorded != 0), 1, 0).astype(jnp.int32)
    return (node_place, shot_place, live_mask)


def draw_live_mask(key, part):
    return geometry(key)[2]


def draw_node_place(key, part):
    return geometry(key)[0]


def draw_shot_place(key, part):
    return geometry(key)[1]


def steps_of(key, shape, shards, smallest, largest):
    loudness, own = 1.0, jax.random.fold_in(key, 6)
    for position, parts in shards:
        steps = jnp.exp(jax.random.uniform(jax.random.fold_in(own, position), (parts,), jnp.float32, smallest / len(shards), largest / len(shards)))
        loudness = loudness * jnp.repeat(steps, shape[position] // parts).reshape([-1 if axis == position else 1 for axis in range(len(shape))])
    return loudness


def bell_draw(own_key, shape, scale, reach, split=(), dtype=jnp.bfloat16):
    entries = scale * jax.random.normal(own_key, shape, jnp.float32)
    if split:
        entries = entries * steps_of(own_key, shape, split, -0.22, 0.18)
    return jnp.clip(entries, -reach, reach).astype(dtype)


def setup_inputs(seed: int = 0) -> dict:
    splits = jax.random.split(jax.random.key(seed), 7)
    return {
        "records": bell_draw(splits[0], (SHOTS, C, NODES, TIME), 1.0, 6.0, ((0, 128), (3, 4))),
        "fan_taps": bell_draw(splits[1], (C, TAPS, TAPS), 0.0667, 0.29882812),
        "dip_taps": bell_draw(splits[2], (TAPS, TAPS), 0.0667, 0.29882812),
        "live_mask": draw_live_mask(jax.random.fold_in(splits[6], 71), 0),
        "node_place": draw_node_place(jax.random.fold_in(splits[6], 71), 0),
        "shot_place": draw_shot_place(jax.random.fold_in(splits[6], 71), 0),
    }


def fan_block(block_data, fan_kernel):
    half = (TAPS - 1) // 2
    return lax.conv_general_dilated(block_data.astype(jnp.float32), fan_kernel, window_strides=(1, 1), padding=((half, half), (half, half)), dimension_numbers=("NCHW", "OIHW", "NCHW"), feature_group_count=C, precision=lax.Precision.HIGHEST)


def dip_block(block_data, dip_kernel):
    half = (TAPS - 1) // 2
    return lax.conv_general_dilated(block_data.astype(jnp.float32), dip_kernel, window_strides=(1, 1), padding=((half, half), (half, half)), dimension_numbers=("NCHW", "OIHW", "NCHW"), precision=lax.Precision.HIGHEST)


def reference(records, fan_taps, dip_taps, live_mask, node_place, shot_place):
    node_order = jnp.argsort(node_place).astype(jnp.int32)
    shot_order = jnp.argsort(shot_place).astype(jnp.int32)
    ordered = jnp.take(records, node_order, axis=2)
    fan_kernel = fan_taps.astype(jnp.float32)[:, None]
    blocks = ordered.reshape(SHOTS // 8, 8, C, NODES, TIME)
    fan_field = lax.map(lambda block_data: fan_block(block_data, fan_kernel), blocks).reshape(SHOTS, C, NODES, TIME)
    live_sorted = jnp.take(live_mask, node_order, axis=1).astype(jnp.float32)
    fanned = (fan_field * live_sorted[:, None, :, None]).astype(jnp.bfloat16)
    gathered = jnp.take(fanned, shot_order, axis=0)
    node_lines = gathered.transpose(1, 2, 0, 3).reshape(C * NODES // 8, 8, 1, SHOTS, TIME)
    dip_kernel = dip_taps.astype(jnp.float32)[None, None]
    filtered = lax.map(lambda block_data: dip_block(block_data, dip_kernel), node_lines)
    filtered = filtered.reshape(C, NODES, SHOTS, TIME).transpose(2, 0, 1, 3)
    return filtered.astype(jnp.bfloat16)
```

```python
import functools

import jax
import jax.numpy as jnp
from jax import lax
from jax.experimental import pallas as pl
from jax.experimental.pallas import tpu as pltpu
from jax.sharding import PartitionSpec as P

LANES = 128
EXT = 256


def time_halo(block, axis, width):
    count = lax.axis_size(axis)
    forward = [(i, i + 1) for i in range(count - 1)]
    backward = [(target, source) for source, target in forward]
    samples = block.shape[-1]
    low = lax.ppermute(lax.slice_in_dim(block, samples - width, None, axis=-1), axis, forward)
    high = lax.ppermute(lax.slice_in_dim(block, 0, width, axis=-1), axis, backward)
    return low, high


def extend(block, low, high, extra=None):
    parts = [block, low, high]
    if extra is not None:
        parts.append(extra)
    used = sum(p.shape[-1] for p in parts)
    pad = jnp.zeros(block.shape[:-1] + (EXT - used,), block.dtype)
    return jnp.concatenate(parts + [pad], axis=-1)


def toeplitz(tap_set, samples, width):
    taps = tap_set.shape[-1]
    j = jnp.arange(EXT, dtype=jnp.int32)
    time_of = jnp.where(
        j < samples,
        j,
        jnp.where(j < samples + width, j - samples - width, jnp.where(j < samples + 2 * width, j - width, 1 << 20)),
    )
    t = jnp.arange(samples, dtype=jnp.int32)
    b = time_of[:, None] - t[None, :] + width
    onehot = (b[:, :, None] == jnp.arange(taps, dtype=jnp.int32)[None, None, :]).astype(jnp.bfloat16)
    tables = jnp.einsum("gab,jtb->gajt", tap_set, onehot, preferred_element_type=jnp.float32)
    return tables.astype(jnp.bfloat16)


def fan_kernel(place_ref, ext_ref, table_ref, out_ref, scr_ref, *, taps, live_col):
    rows = ext_ref.shape[1]
    reach = (taps - 1) // 2
    place = place_ref[...]
    select = (lax.broadcasted_iota(jnp.int32, (rows, rows), 0) == place).astype(jnp.bfloat16)
    ordered = jnp.dot(select, ext_ref[0], preferred_element_type=jnp.float32)
    keep = ordered[:, live_col:live_col + 1]
    ordered = ordered.astype(jnp.bfloat16)
    scr_ref[0:8, :] = jnp.zeros((8, LANES), jnp.float32)
    scr_ref[rows + 8:rows + 16, :] = jnp.zeros((8, LANES), jnp.float32)
    acc = jnp.zeros((rows, LANES), jnp.float32)
    for a in range(taps):
        part = jnp.dot(ordered, table_ref[0, a], preferred_element_type=jnp.float32)
        scr_ref[8:rows + 8, :] = part
        acc = acc + scr_ref[pl.ds(a + 8 - reach, rows), :]
    out_ref[0] = (acc * keep).astype(out_ref.dtype)


def dip_kernel(target_ref, ext_ref, table_ref, out_ref, scr_ref, *, taps, group):
    rows = ext_ref.shape[1]
    reach = (taps - 1) // 2
    pad = group * 8
    target = target_ref[...]
    select = (lax.broadcasted_iota(jnp.int32, (rows, rows), 0) == target).astype(jnp.bfloat16)
    ordered = jnp.dot(select, ext_ref[0], preferred_element_type=jnp.float32).astype(jnp.bfloat16)
    scr_ref[0:pad, :] = jnp.zeros((pad, LANES), jnp.float32)
    scr_ref[rows + pad:rows + 2 * pad, :] = jnp.zeros((pad, LANES), jnp.float32)
    acc = jnp.zeros((rows, LANES), jnp.float32)
    for a in range(taps):
        part = jnp.dot(ordered, table_ref[a], preferred_element_type=jnp.float32)
        scr_ref[pad:rows + pad, :] = part
        acc = acc + scr_ref[pl.ds(pad + group * (a - reach), rows), :]
    out_ref[0] = acc.astype(out_ref.dtype)


def fan_call(place, ext, tables):
    comps, rows, _ = ext.shape
    taps = tables.shape[1]
    samples = tables.shape[3]
    kernel = functools.partial(fan_kernel, taps=taps, live_col=samples + taps - 1)
    return pl.pallas_call(
        kernel,
        grid=(comps,),
        in_specs=[
            pl.BlockSpec((1, rows), lambda c: (0, 0)),
            pl.BlockSpec((1, rows, EXT), lambda c: (c, 0, 0)),
            pl.BlockSpec((1, taps, EXT, samples), lambda c: (c, 0, 0, 0)),
        ],
        out_specs=pl.BlockSpec((1, rows, samples), lambda c: (c, 0, 0)),
        out_shape=jax.ShapeDtypeStruct((comps, rows, samples), jnp.bfloat16),
        scratch_shapes=[pltpu.VMEM((rows + 16, LANES), jnp.float32)],
    )(place, ext, tables)


def dip_call(target, ext, tables, group):
    comps, rows, _ = ext.shape
    taps = tables.shape[0]
    samples = tables.shape[2]
    kernel = functools.partial(dip_kernel, taps=taps, group=group)
    return pl.pallas_call(
        kernel,
        grid=(comps,),
        in_specs=[
            pl.BlockSpec((1, rows), lambda c: (0, 0)),
            pl.BlockSpec((1, rows, EXT), lambda c: (c, 0, 0)),
            pl.BlockSpec((taps, EXT, samples), lambda c: (0, 0, 0)),
        ],
        out_specs=pl.BlockSpec((1, rows, samples), lambda c: (c, 0, 0)),
        out_shape=jax.ShapeDtypeStruct((comps, rows, samples), jnp.bfloat16),
        scratch_shapes=[pltpu.VMEM((rows + 16 * group, LANES), jnp.float32)],
    )(target, ext, tables)


def on_device(records, fan_taps, dip_taps, live_mask, node_place, shot_place):
    _, comps, nodes, samples = records.shape
    taps = fan_taps.shape[1]
    reach = (taps - 1) // 2
    devices = lax.axis_size("shot")
    group = nodes // devices

    block = records[0]
    low, high = time_halo(block, "tm", reach)
    live = jnp.broadcast_to(live_mask[0].astype(jnp.bfloat16)[None, :, None], (comps, nodes, 1))
    ext = extend(block, low, high, live)
    fanned = fan_call(node_place[None, :], ext, toeplitz(fan_taps, samples, reach))

    sent = fanned.reshape(comps, devices, group, samples).transpose(1, 0, 2, 3)
    arrived = lax.all_to_all(sent, "shot", split_axis=0, concat_axis=0, tiled=True)
    lines = arrived.transpose(1, 0, 2, 3)
    low, high = time_halo(lines, "tm", reach)
    ext2 = extend(lines, low, high).reshape(comps, devices * group, EXT)
    target = (jnp.repeat(shot_place, group) * group + jnp.tile(jnp.arange(group, dtype=jnp.int32), devices))[None, :]
    tables = toeplitz(dip_taps[None], samples, reach)[0]
    out = dip_call(target, ext2, tables, group)
    return out.reshape(comps, devices, group, samples).transpose(1, 0, 2, 3)


def solution(mesh):
    return jax.shard_map(
        on_device,
        mesh=mesh,
        in_specs=(P("shot", None, None, "tm"), P(), P(), P("shot", None), P(), P()),
        out_specs=P(None, None, "shot", "tm"),
        check_vma=False,
    )
```

```python
import functools

import jax
import jax.numpy as jnp
from jax import lax
from jax.experimental import pallas as pl
from jax.experimental.pallas import tpu as pltpu
from jax.sharding import PartitionSpec as P

LANES = 128
EXT = 256


def time_halo(block, axis, width):
    count = lax.axis_size(axis)
    forward = [(i, i + 1) for i in range(count - 1)]
    backward = [(target, source) for source, target in forward]
    samples = block.shape[-1]
    low = lax.ppermute(lax.slice_in_dim(block, samples - width, None, axis=-1), axis, forward)
    high = lax.ppermute(lax.slice_in_dim(block, 0, width, axis=-1), axis, backward)
    return low, high


def extend(block, low, high, extra=None):
    parts = [block, low, high]
    if extra is not None:
        parts.append(extra)
    used = sum(p.shape[-1] for p in parts)
    pad = jnp.zeros(block.shape[:-1] + (EXT - used,), block.dtype)
    return jnp.concatenate(parts + [pad], axis=-1)


def toeplitz(tap_set, samples, width):
    taps = tap_set.shape[-1]
    j = jnp.arange(EXT, dtype=jnp.int32)
    time_of = jnp.where(
        j < samples,
        j,
        jnp.where(j < samples + width, j - samples - width, jnp.where(j < samples + 2 * width, j - width, 1 << 20)),
    )
    t = jnp.arange(samples, dtype=jnp.int32)
    b = time_of[:, None] - t[None, :] + width
    onehot = (b[:, :, None] == jnp.arange(taps, dtype=jnp.int32)[None, None, :]).astype(jnp.bfloat16)
    tables = jnp.einsum("gab,jtb->gajt", tap_set, onehot, preferred_element_type=jnp.float32)
    return tables.astype(jnp.bfloat16)


def fan_tables(fan_taps, samples, reach):
    comps, _, taps = fan_taps.shape
    wide = 2 * reach
    j = jnp.arange(EXT, dtype=jnp.int32)
    time_of = jnp.where(
        j < samples,
        j,
        jnp.where(j < samples + wide, j - samples - wide, jnp.where(j < samples + 2 * wide, j - wide, 1 << 20)),
    )
    col = jnp.arange(EXT, dtype=jnp.int32)
    k = col - samples
    owner = k // wide
    r = k % wide
    halo_t = jnp.where(r < reach, r - reach, samples - reach + r)
    c = jnp.arange(comps, dtype=jnp.int32)[:, None]
    t_of = jnp.where(col[None, :] < samples, col[None, :], jnp.where((owner[None, :] == c) & (k[None, :] < comps * wide), halo_t[None, :], -(1 << 20)))
    b = time_of[None, :, None] - t_of[:, None, :] + reach
    onehot = (b[..., None] == jnp.arange(taps, dtype=jnp.int32)).astype(jnp.bfloat16)
    tables = jnp.einsum("gab,gjtb->gajt", fan_taps, onehot, preferred_element_type=jnp.float32)
    return tables.astype(jnp.bfloat16)


def fan_kernel(place_ref, edge_ref, ext_ref, table_ref, out_ref, scr_ref, halo_ref, *, taps, live_col):
    c = pl.program_id(0)
    rows = ext_ref.shape[1]
    samples = LANES
    place = place_ref[...]
    select = (lax.broadcasted_iota(jnp.int32, (rows, rows), 0) == place).astype(jnp.bfloat16)
    ordered = jnp.dot(select, ext_ref[0], preferred_element_type=jnp.float32)
    keep = ordered[:, live_col:live_col + 1]
    ordered = ordered.astype(jnp.bfloat16)
    scr_ref[0:8, :] = jnp.zeros((8, EXT), jnp.float32)
    scr_ref[rows + 8:rows + 16, :] = jnp.zeros((8, EXT), jnp.float32)
    acc = jnp.zeros((rows, EXT), jnp.float32)
    for a in range(taps):
        part = jnp.dot(ordered, table_ref[0, a], preferred_element_type=jnp.float32)
        scr_ref[8:rows + 8, :] = part
        acc = acc + scr_ref[pl.ds(a + 1, rows), :]
    out_ref[:, pl.ds(pl.multiple_of(c * samples, samples), samples)] = (acc[:, :samples] * keep).astype(out_ref.dtype)

    @pl.when(c == 0)
    def _():
        halo_ref[...] = acc[:, samples:]

    @pl.when(c > 0)
    def _():
        halo_ref[...] += acc[:, samples:]

    @pl.when(c == pl.num_programs(0) - 1)
    def _():
        out_ref[:, pl.ds(pl.num_programs(0) * samples, samples)] = (halo_ref[...] * keep * edge_ref[...]).astype(out_ref.dtype)


def dip_kernel(target_ref, data_ref, table_ref, out_ref, scr_ref, *, taps, group, comps, reach):
    rows = data_ref.shape[0]
    samples = LANES
    pad = group * 8
    target = target_ref[...]
    select = (lax.broadcasted_iota(jnp.int32, (rows, rows), 0) == target).astype(jnp.bfloat16)
    halo = jnp.dot(select, data_ref[:, comps * samples:(comps + 1) * samples], preferred_element_type=jnp.float32)
    scr_ref[0:pad, :] = jnp.zeros((pad, LANES), jnp.float32)
    scr_ref[rows + pad:rows + 2 * pad, :] = jnp.zeros((pad, LANES), jnp.float32)
    for c in range(comps):
        main = jnp.dot(select, data_ref[:, c * samples:(c + 1) * samples], preferred_element_type=jnp.float32)
        mine = halo if c == 0 else pltpu.roll(halo, samples - 2 * reach * c, 1)
        ordered = jnp.concatenate([main, mine], axis=1).astype(jnp.bfloat16)
        acc = jnp.zeros((rows, LANES), jnp.float32)
        for a in range(taps):
            part = jnp.dot(ordered, table_ref[a], preferred_element_type=jnp.float32)
            scr_ref[pad:rows + pad, :] = part
            acc = acc + scr_ref[pl.ds(pad + group * (a - reach), rows), :]
        out_ref[c] = acc.astype(out_ref.dtype)


def fan_call(place, edge, ext, tables):
    comps, rows, _ = ext.shape
    taps = tables.shape[1]
    kernel = functools.partial(fan_kernel, taps=taps, live_col=LANES + 2 * (taps - 1))
    return pl.pallas_call(
        kernel,
        grid=(comps,),
        in_specs=[
            pl.BlockSpec((1, rows), lambda c: (0, 0)),
            pl.BlockSpec((1, LANES), lambda c: (0, 0)),
            pl.BlockSpec((1, rows, EXT), lambda c: (c, 0, 0)),
            pl.BlockSpec((1, taps, EXT, EXT), lambda c: (c, 0, 0, 0)),
        ],
        out_specs=pl.BlockSpec((rows, (comps + 1) * LANES), lambda c: (0, 0)),
        out_shape=jax.ShapeDtypeStruct((rows, (comps + 1) * LANES), jnp.bfloat16),
        scratch_shapes=[pltpu.VMEM((rows + 16, EXT), jnp.float32), pltpu.VMEM((rows, LANES), jnp.float32)],
    )(place, edge, ext, tables)


def dip_call(target, data, tables, group, comps, reach):
    rows = data.shape[0]
    taps = tables.shape[0]
    kernel = functools.partial(dip_kernel, taps=taps, group=group, comps=comps, reach=reach)
    return pl.pallas_call(
        kernel,
        out_shape=jax.ShapeDtypeStruct((comps, rows, LANES), jnp.bfloat16),
        scratch_shapes=[pltpu.VMEM((rows + 16 * group, LANES), jnp.float32)],
    )(target, data, tables)


def on_device(records, fan_taps, dip_taps, live_mask, node_place, shot_place):
    _, comps, nodes, samples = records.shape
    taps = fan_taps.shape[1]
    reach = (taps - 1) // 2
    devices = lax.axis_size("shot")
    group = nodes // devices

    block = records[0]
    low, high = time_halo(block, "tm", 2 * reach)
    live = jnp.broadcast_to(live_mask[0].astype(jnp.bfloat16)[None, :, None], (comps, nodes, 1))
    ext = extend(block, low, high, live)
    place = lax.axis_index("tm")
    lane = jnp.arange(LANES, dtype=jnp.int32) % (2 * reach)
    edge = jnp.where(lane < reach, place > 0, place < lax.axis_size("tm") - 1).astype(jnp.float32)[None, :]
    packed = fan_call(node_place[None, :], edge, ext, fan_tables(fan_taps, samples, reach))

    sent = packed.reshape(devices, group, packed.shape[-1])
    arrived = lax.all_to_all(sent, "shot", split_axis=0, concat_axis=0, tiled=True)
    data = arrived.reshape(devices * group, packed.shape[-1])
    target = (jnp.repeat(shot_place, group) * group + jnp.tile(jnp.arange(group, dtype=jnp.int32), devices))[None, :]
    tables = toeplitz(dip_taps[None], samples, reach)[0]
    out = dip_call(target, data, tables, group, comps, reach)
    return out.reshape(comps, devices, group, samples).transpose(1, 0, 2, 3)


def solution(mesh):
    return jax.shard_map(
        on_device,
        mesh=mesh,
        in_specs=(P("shot", None, None, "tm"), P(), P(), P("shot", None), P(), P()),
        out_specs=P(None, None, "shot", "tm"),
        check_vma=False,
    )
```

```python
import functools

import jax
import jax.numpy as jnp
from jax import lax
from jax.experimental import pallas as pl
from jax.experimental.pallas import tpu as pltpu
from jax.sharding import PartitionSpec as P

LANES = 128
EXT = 256


def time_halo(block, axis, width):
    count = lax.axis_size(axis)
    forward = [(i, i + 1) for i in range(count - 1)]
    backward = [(target, source) for source, target in forward]
    samples = block.shape[-1]
    low = lax.ppermute(lax.slice_in_dim(block, samples - width, None, axis=-1), axis, forward)
    high = lax.ppermute(lax.slice_in_dim(block, 0, width, axis=-1), axis, backward)
    return low, high


def circulant(tap_set, samples):
    taps = tap_set.shape[-1]
    reach = (taps - 1) // 2
    j = jnp.arange(EXT, dtype=jnp.int32)
    t = jnp.arange(samples, dtype=jnp.int32)
    b = (j[:, None] - t[None, :] + reach) % EXT
    onehot = (b[:, :, None] == jnp.arange(taps, dtype=jnp.int32)[None, None, :]).astype(jnp.bfloat16)
    tables = jnp.einsum("gab,jtb->gajt", tap_set, onehot, preferred_element_type=jnp.float32)
    return tables.astype(jnp.bfloat16)


def fan_kernel(place_ref, edge_ref, ext_ref, table_ref, out_ref, scr_ref, halo_ref, *, taps, live_col, comps):
    c = pl.program_id(0)
    rows = ext_ref.shape[1]
    samples = LANES
    reach = (taps - 1) // 2
    place = place_ref[...]
    select = (lax.broadcasted_iota(jnp.int32, (rows, rows), 0) == place).astype(jnp.bfloat16)
    ordered = jnp.dot(select, ext_ref[0], preferred_element_type=jnp.float32)
    keep = ordered[:, live_col:live_col + 1]
    ordered = ordered.astype(jnp.bfloat16)
    swapped = jnp.concatenate([ordered[:, samples:], ordered[:, :samples]], axis=1)
    second = rows + 16
    zeros = jnp.zeros((8, LANES), jnp.float32)
    scr_ref[0:8, :] = zeros
    scr_ref[rows + 8:rows + 16, :] = zeros
    scr_ref[second + rows:second + rows + 8, :] = zeros
    acc = jnp.zeros((rows, LANES), jnp.float32)
    acc_h = jnp.zeros((rows, LANES), jnp.float32)
    for a in range(taps):
        table = table_ref[0, a]
        scr_ref[8:rows + 8, :] = jnp.dot(ordered, table, preferred_element_type=jnp.float32)
        scr_ref[second:second + rows, :] = jnp.dot(swapped, table, preferred_element_type=jnp.float32)
        acc = acc + scr_ref[pl.ds(a + 8 - reach, rows), :]
        acc_h = acc_h + scr_ref[pl.ds(second + a - reach, rows), :]
    out_ref[:, pl.ds(pl.multiple_of(c * samples, samples), samples)] = (acc * keep).astype(out_ref.dtype)
    lane = lax.broadcasted_iota(jnp.int32, (rows, LANES), 1)
    for k in range(comps):
        @pl.when(c == k)
        def _():
            moved = pltpu.roll(acc_h, reach + 2 * reach * k, 1)
            mine = jnp.where((lane >= 2 * reach * k) & (lane < 2 * reach * (k + 1)), moved, 0.0)
            if k == 0:
                halo_ref[...] = mine
            else:
                halo_ref[...] += mine

    @pl.when(c == comps - 1)
    def _():
        out_ref[:, comps * samples:(comps + 1) * samples] = (halo_ref[...] * keep * edge_ref[...]).astype(out_ref.dtype)


def dip_kernel(target_ref, data_ref, table_ref, out_ref, scr_ref, *, taps, group, comps):
    rows = data_ref.shape[0]
    samples = LANES
    reach = (taps - 1) // 2
    pad = group * 8
    target = target_ref[...]
    select = (lax.broadcasted_iota(jnp.int32, (rows, rows), 0) == target).astype(jnp.bfloat16)
    halo = jnp.dot(select, data_ref[:, comps * samples:(comps + 1) * samples], preferred_element_type=jnp.float32)
    scr_ref[0:pad, :] = jnp.zeros((pad, LANES), jnp.float32)
    scr_ref[rows + pad:rows + 2 * pad, :] = jnp.zeros((pad, LANES), jnp.float32)
    for c in range(comps):
        main = jnp.dot(select, data_ref[:, c * samples:(c + 1) * samples], preferred_element_type=jnp.float32)
        mine = pltpu.roll(halo, (samples - reach - 2 * reach * c) % samples, 1)
        ordered = jnp.concatenate([main, mine], axis=1).astype(jnp.bfloat16)
        acc = jnp.zeros((rows, LANES), jnp.float32)
        for a in range(taps):
            part = jnp.dot(ordered, table_ref[0, a], preferred_element_type=jnp.float32)
            scr_ref[pad:rows + pad, :] = part
            acc = acc + scr_ref[pl.ds(pad + group * (a - reach), rows), :]
        out_ref[c] = acc.astype(out_ref.dtype)


def fan_call(place, edge, ext, tables, live_col):
    comps, rows, _ = ext.shape
    taps = tables.shape[1]
    kernel = functools.partial(fan_kernel, taps=taps, live_col=live_col, comps=comps)
    return pl.pallas_call(
        kernel,
        grid=(comps,),
        in_specs=[
            pl.BlockSpec((1, rows), lambda c: (0, 0)),
            pl.BlockSpec((1, LANES), lambda c: (0, 0)),
            pl.BlockSpec((1, rows, EXT), lambda c: (c, 0, 0)),
            pl.BlockSpec((1, taps, EXT, LANES), lambda c: (c, 0, 0, 0)),
        ],
        out_specs=pl.BlockSpec((rows, (comps + 1) * LANES), lambda c: (0, 0)),
        out_shape=jax.ShapeDtypeStruct((rows, (comps + 1) * LANES), jnp.bfloat16),
        scratch_shapes=[pltpu.VMEM((2 * rows + 24, LANES), jnp.float32), pltpu.VMEM((rows, LANES), jnp.float32)],
    )(place, edge, ext, tables)


def dip_call(target, data, tables, group, comps):
    rows = data.shape[0]
    taps = tables.shape[1]
    kernel = functools.partial(dip_kernel, taps=taps, group=group, comps=comps)
    return pl.pallas_call(
        kernel,
        out_shape=jax.ShapeDtypeStruct((comps, rows, LANES), jnp.bfloat16),
        scratch_shapes=[pltpu.VMEM((rows + 16 * group, LANES), jnp.float32)],
    )(target, data, tables)


def on_device(records, fan_taps, dip_taps, live_mask, node_place, shot_place):
    _, comps, nodes, samples = records.shape
    taps = fan_taps.shape[1]
    reach = (taps - 1) // 2
    wide = 2 * reach
    devices = lax.axis_size("shot")
    group = nodes // devices

    block = records[0]
    low, high = time_halo(block, "tm", wide)
    live_col = samples + 32
    live = jnp.broadcast_to(live_mask[0].astype(jnp.bfloat16)[None, :, None], (comps, nodes, 1))
    gap1 = jnp.zeros((comps, nodes, live_col - samples - wide), jnp.bfloat16)
    gap2 = jnp.zeros((comps, nodes, EXT - wide - live_col - 1), jnp.bfloat16)
    ext = jnp.concatenate([block, high, gap1, live, gap2, low], axis=-1)
    place = lax.axis_index("tm")
    lane = jnp.arange(LANES, dtype=jnp.int32) % wide
    edge = jnp.where(lane < reach, place > 0, place < lax.axis_size("tm") - 1).astype(jnp.float32)[None, :]
    packed = fan_call(node_place[None, :], edge, ext, circulant(fan_taps, samples), live_col)

    sent = packed.reshape(devices, group, packed.shape[-1])
    arrived = lax.all_to_all(sent, "shot", split_axis=0, concat_axis=0, tiled=True)
    data = arrived.reshape(devices * group, packed.shape[-1])
    target = (jnp.repeat(shot_place, group) * group + jnp.tile(jnp.arange(group, dtype=jnp.int32), devices))[None, :]
    out = dip_call(target, data, circulant(dip_taps[None], samples), group, comps)
    return out.reshape(comps, devices, group, samples).transpose(1, 0, 2, 3)


def solution(mesh):
    return jax.shard_map(
        on_device,
        mesh=mesh,
        in_specs=(P("shot", None, None, "tm"), P(), P(), P("shot", None), P(), P()),
        out_specs=P(None, None, "shot", "tm"),
        check_vma=False,
    )
```

```python
import functools

import jax
import jax.numpy as jnp
from jax import lax
from jax.experimental import pallas as pl
from jax.experimental.pallas import tpu as pltpu
from jax.sharding import PartitionSpec as P

LANES = 128
EXT = 256


def time_halo(block, axis, width):
    count = lax.axis_size(axis)
    forward = [(i, i + 1) for i in range(count - 1)]
    backward = [(target, source) for source, target in forward]
    samples = block.shape[-1]
    low = lax.ppermute(lax.slice_in_dim(block, samples - width, None, axis=-1), axis, forward)
    high = lax.ppermute(lax.slice_in_dim(block, 0, width, axis=-1), axis, backward)
    return low, high


def circulant(tap_set, samples):
    taps = tap_set.shape[-1]
    reach = (taps - 1) // 2
    j = jnp.arange(EXT, dtype=jnp.int32)
    t = jnp.arange(samples, dtype=jnp.int32)
    b = (j[:, None] - t[None, :] + reach) % EXT
    onehot = (b[:, :, None] == jnp.arange(taps, dtype=jnp.int32)[None, None, :]).astype(jnp.bfloat16)
    tables = jnp.einsum("gab,jtb->jgat", tap_set, onehot, preferred_element_type=jnp.float32)
    return tables.astype(jnp.bfloat16)


def fan_kernel(place_ref, edge_ref, ext_ref, table_ref, out_ref, scr_ref, halo_ref, *, taps, live_col, comps):
    c = pl.program_id(0)
    rows = ext_ref.shape[1]
    samples = LANES
    reach = (taps - 1) // 2
    place = place_ref[...]
    select = (lax.broadcasted_iota(jnp.int32, (rows, rows), 0) == place).astype(jnp.bfloat16)
    ordered = jnp.dot(select, ext_ref[0], preferred_element_type=jnp.float32)
    keep = ordered[:, live_col:live_col + 1]
    ordered = ordered.astype(jnp.bfloat16)
    swapped = jnp.concatenate([ordered[:, samples:], ordered[:, :samples]], axis=1)
    second = rows + 16
    zeros = jnp.zeros((8, LANES), jnp.float32)
    scr_ref[0:8, :] = zeros
    scr_ref[rows + 8:rows + 16, :] = zeros
    scr_ref[second + rows:second + rows + 8, :] = zeros
    acc = jnp.zeros((rows, LANES), jnp.float32)
    acc_h = jnp.zeros((rows, LANES), jnp.float32)
    for a in range(taps):
        table = table_ref[:, 0, a, :]
        scr_ref[8:rows + 8, :] = jnp.dot(ordered, table, preferred_element_type=jnp.float32)
        scr_ref[second:second + rows, :] = jnp.dot(swapped, table, preferred_element_type=jnp.float32)
        acc = acc + scr_ref[pl.ds(a + 8 - reach, rows), :]
        acc_h = acc_h + scr_ref[pl.ds(second + a - reach, rows), :]
    out_ref[:, pl.ds(pl.multiple_of(c * samples, samples), samples)] = (acc * keep).astype(out_ref.dtype)
    lane = lax.broadcasted_iota(jnp.int32, (rows, LANES), 1)
    for k in range(comps):
        @pl.when(c == k)
        def _():
            moved = pltpu.roll(acc_h, reach + 2 * reach * k, 1)
            mine = jnp.where((lane >= 2 * reach * k) & (lane < 2 * reach * (k + 1)), moved, 0.0)
            if k == 0:
                halo_ref[...] = mine
            else:
                halo_ref[...] += mine

    @pl.when(c == comps - 1)
    def _():
        out_ref[:, comps * samples:(comps + 1) * samples] = (halo_ref[...] * keep * edge_ref[...]).astype(out_ref.dtype)


def dip_kernel(target_ref, data_ref, table_ref, out_ref, scr_ref, *, taps, group, comps):
    rows = data_ref.shape[0]
    samples = LANES
    reach = (taps - 1) // 2
    pad = group * 8
    target = target_ref[...]
    select = (lax.broadcasted_iota(jnp.int32, (rows, rows), 0) == target).astype(jnp.bfloat16)
    halo = jnp.dot(select, data_ref[:, comps * samples:(comps + 1) * samples], preferred_element_type=jnp.float32)
    scr_ref[0:pad, :] = jnp.zeros((pad, LANES), jnp.float32)
    scr_ref[rows + pad:rows + 2 * pad, :] = jnp.zeros((pad, LANES), jnp.float32)
    for c in range(comps):
        main = jnp.dot(select, data_ref[:, c * samples:(c + 1) * samples], preferred_element_type=jnp.float32)
        mine = pltpu.roll(halo, (samples - reach - 2 * reach * c) % samples, 1)
        ordered = jnp.concatenate([main, mine], axis=1).astype(jnp.bfloat16)
        acc = jnp.zeros((rows, LANES), jnp.float32)
        for a in range(taps):
            part = jnp.dot(ordered, table_ref[:, 0, a, :], preferred_element_type=jnp.float32)
            scr_ref[pad:rows + pad, :] = part
            acc = acc + scr_ref[pl.ds(pad + group * (a - reach), rows), :]
        out_ref[c] = acc.astype(out_ref.dtype)


def fan_call(place, edge, ext, tables, live_col):
    comps, rows, _ = ext.shape
    taps = tables.shape[2]
    kernel = functools.partial(fan_kernel, taps=taps, live_col=live_col, comps=comps)
    return pl.pallas_call(
        kernel,
        grid=(comps,),
        in_specs=[
            pl.BlockSpec((1, rows), lambda c: (0, 0)),
            pl.BlockSpec((1, LANES), lambda c: (0, 0)),
            pl.BlockSpec((1, rows, EXT), lambda c: (c, 0, 0)),
            pl.BlockSpec((EXT, 1, taps, LANES), lambda c: (0, c, 0, 0)),
        ],
        out_specs=pl.BlockSpec((rows, (comps + 1) * LANES), lambda c: (0, 0)),
        out_shape=jax.ShapeDtypeStruct((rows, (comps + 1) * LANES), jnp.bfloat16),
        scratch_shapes=[pltpu.VMEM((2 * rows + 24, LANES), jnp.float32), pltpu.VMEM((rows, LANES), jnp.float32)],
    )(place, edge, ext, tables)


def dip_call(target, data, tables, group, comps):
    rows = data.shape[0]
    taps = tables.shape[2]
    kernel = functools.partial(dip_kernel, taps=taps, group=group, comps=comps)
    return pl.pallas_call(
        kernel,
        out_shape=jax.ShapeDtypeStruct((comps, rows, LANES), jnp.bfloat16),
        scratch_shapes=[pltpu.VMEM((rows + 16 * group, LANES), jnp.float32)],
    )(target, data, tables)


def on_device(records, fan_taps, dip_taps, live_mask, node_place, shot_place):
    _, comps, nodes, samples = records.shape
    taps = fan_taps.shape[1]
    reach = (taps - 1) // 2
    wide = 2 * reach
    devices = lax.axis_size("shot")
    group = nodes // devices

    block = records[0]
    low, high = time_halo(block, "tm", wide)
    live_col = samples + 32
    live = jnp.broadcast_to(live_mask[0].astype(jnp.bfloat16)[None, :, None], (comps, nodes, 1))
    gap1 = jnp.zeros((comps, nodes, live_col - samples - wide), jnp.bfloat16)
    gap2 = jnp.zeros((comps, nodes, EXT - wide - live_col - 1), jnp.bfloat16)
    ext = jnp.concatenate([block, high, gap1, live, gap2, low], axis=-1)
    place = lax.axis_index("tm")
    lane = jnp.arange(LANES, dtype=jnp.int32) % wide
    edge = jnp.where(lane < reach, place > 0, place < lax.axis_size("tm") - 1).astype(jnp.float32)[None, :]
    packed = fan_call(node_place[None, :], edge, ext, circulant(fan_taps, samples), live_col)

    sent = packed.reshape(devices, group, packed.shape[-1])
    arrived = lax.all_to_all(sent, "shot", split_axis=0, concat_axis=0, tiled=True)
    data = arrived.reshape(devices * group, packed.shape[-1])
    target = (jnp.repeat(shot_place, group) * group + jnp.tile(jnp.arange(group, dtype=jnp.int32), devices))[None, :]
    out = dip_call(target, data, circulant(dip_taps[None], samples), group, comps)
    return out.reshape(comps, devices, group, samples).transpose(1, 0, 2, 3)


def solution(mesh):
    return jax.shard_map(
        on_device,
        mesh=mesh,
        in_specs=(P("shot", None, None, "tm"), P(), P(), P("shot", None), P(), P()),
        out_specs=P(None, None, "shot", "tm"),
        check_vma=False,
    )
```

```python
import functools

import jax
import jax.numpy as jnp
from jax import lax
from jax.experimental import pallas as pl
from jax.experimental.pallas import tpu as pltpu
from jax.sharding import PartitionSpec as P

LANES = 128
EXT = 256


def time_halo(block, axis, width):
    count = lax.axis_size(axis)
    forward = [(i, i + 1) for i in range(count - 1)]
    backward = [(target, source) for source, target in forward]
    samples = block.shape[-1]
    low = lax.ppermute(lax.slice_in_dim(block, samples - width, None, axis=-1), axis, forward)
    high = lax.ppermute(lax.slice_in_dim(block, 0, width, axis=-1), axis, backward)
    return low, high


def circulant(tap_set, samples):
    taps = tap_set.shape[-1]
    reach = (taps - 1) // 2
    j = jnp.arange(EXT, dtype=jnp.int32)
    t = jnp.arange(samples, dtype=jnp.int32)
    b = (j[:, None] - t[None, :] + reach) % EXT
    onehot = (b[:, :, None] == jnp.arange(taps, dtype=jnp.int32)[None, None, :]).astype(jnp.bfloat16)
    tables = jnp.einsum("gab,jtb->gajt", tap_set, onehot, preferred_element_type=jnp.float32)
    return tables.astype(jnp.bfloat16)


def fan_kernel(place_ref, edge_ref, live_ref, block_ref, prev_ref, next_ref, table_ref, out_ref, scr_ref, halo_ref, *, taps, comps):
    c = pl.program_id(0)
    rows = block_ref.shape[1]
    samples = LANES
    reach = (taps - 1) // 2
    wide = 2 * reach
    place = place_ref[...]
    select = (lax.broadcasted_iota(jnp.int32, (rows, rows), 0) == place).astype(jnp.bfloat16)
    keep = jnp.sum(select.astype(jnp.float32) * live_ref[...].astype(jnp.float32), axis=1, keepdims=True)
    lane = lax.broadcasted_iota(jnp.int32, (rows, LANES), 1)
    outer = jnp.where(lane < wide, next_ref[0], jnp.where(lane >= LANES - wide, prev_ref[0], jnp.zeros_like(prev_ref[0])))
    ext = jnp.concatenate([block_ref[0], outer], axis=1)
    ordered = jnp.dot(select, ext, preferred_element_type=jnp.float32).astype(jnp.bfloat16)
    swapped = jnp.concatenate([ordered[:, samples:], ordered[:, :samples]], axis=1)
    second = rows + 16
    zeros = jnp.zeros((8, LANES), jnp.float32)
    scr_ref[0:8, :] = zeros
    scr_ref[rows + 8:rows + 16, :] = zeros
    scr_ref[second + rows:second + rows + 8, :] = zeros
    acc = jnp.zeros((rows, LANES), jnp.float32)
    acc_h = jnp.zeros((rows, LANES), jnp.float32)
    for a in range(taps):
        table = table_ref[0, a]
        scr_ref[8:rows + 8, :] = jnp.dot(ordered, table, preferred_element_type=jnp.float32)
        scr_ref[second:second + rows, :] = jnp.dot(swapped, table, preferred_element_type=jnp.float32)
        acc = acc + scr_ref[pl.ds(a + 8 - reach, rows), :]
        acc_h = acc_h + scr_ref[pl.ds(second + a - reach, rows), :]
    out_ref[:, pl.ds(pl.multiple_of(c * samples, samples), samples)] = (acc * keep).astype(out_ref.dtype)
    for k in range(comps):
        @pl.when(c == k)
        def _():
            moved = pltpu.roll(acc_h, reach + 2 * reach * k, 1)
            mine = jnp.where((lane >= 2 * reach * k) & (lane < 2 * reach * (k + 1)), moved, 0.0)
            if k == 0:
                halo_ref[...] = mine
            else:
                halo_ref[...] += mine

    @pl.when(c == comps - 1)
    def _():
        out_ref[:, comps * samples:(comps + 1) * samples] = (halo_ref[...] * keep * edge_ref[...]).astype(out_ref.dtype)


def dip_kernel(target_ref, data_ref, table_ref, out_ref, scr_ref, *, taps, group, comps):
    rows = data_ref.shape[0]
    samples = LANES
    reach = (taps - 1) // 2
    pad = group * 8
    target = target_ref[...]
    select = (lax.broadcasted_iota(jnp.int32, (rows, rows), 0) == target).astype(jnp.bfloat16)
    halo = jnp.dot(select, data_ref[:, comps * samples:(comps + 1) * samples], preferred_element_type=jnp.float32)
    scr_ref[0:pad, :] = jnp.zeros((pad, LANES), jnp.float32)
    scr_ref[rows + pad:rows + 2 * pad, :] = jnp.zeros((pad, LANES), jnp.float32)
    for c in range(comps):
        main = jnp.dot(select, data_ref[:, c * samples:(c + 1) * samples], preferred_element_type=jnp.float32)
        mine = pltpu.roll(halo, (samples - reach - 2 * reach * c) % samples, 1)
        ordered = jnp.concatenate([main, mine], axis=1).astype(jnp.bfloat16)
        acc = jnp.zeros((rows, LANES), jnp.float32)
        for a in range(taps):
            part = jnp.dot(ordered, table_ref[0, a], preferred_element_type=jnp.float32)
            scr_ref[pad:rows + pad, :] = part
            acc = acc + scr_ref[pl.ds(pad + group * (a - reach), rows), :]
        out_ref[c] = acc.astype(out_ref.dtype)


def fan_call(place, edge, live, block, prev, nxt, tables):
    comps, rows, samples = block.shape
    taps = tables.shape[1]
    kernel = functools.partial(fan_kernel, taps=taps, comps=comps)
    part = pl.BlockSpec((1, rows, samples), lambda c: (c, 0, 0))
    return pl.pallas_call(
        kernel,
        grid=(comps,),
        in_specs=[
            pl.BlockSpec((1, rows), lambda c: (0, 0)),
            pl.BlockSpec((1, LANES), lambda c: (0, 0)),
            pl.BlockSpec((1, rows), lambda c: (0, 0)),
            part,
            part,
            part,
            pl.BlockSpec((1, taps, EXT, LANES), lambda c: (c, 0, 0, 0)),
        ],
        out_specs=pl.BlockSpec((rows, (comps + 1) * LANES), lambda c: (0, 0)),
        out_shape=jax.ShapeDtypeStruct((rows, (comps + 1) * LANES), jnp.bfloat16),
        scratch_shapes=[pltpu.VMEM((2 * rows + 24, LANES), jnp.float32), pltpu.VMEM((rows, LANES), jnp.float32)],
    )(place, edge, live, block, prev, nxt, tables)


def dip_call(target, data, tables, group, comps):
    rows = data.shape[0]
    taps = tables.shape[1]
    kernel = functools.partial(dip_kernel, taps=taps, group=group, comps=comps)
    return pl.pallas_call(
        kernel,
        out_shape=jax.ShapeDtypeStruct((comps, rows, LANES), jnp.bfloat16),
        scratch_shapes=[pltpu.VMEM((rows + 16 * group, LANES), jnp.float32)],
    )(target, data, tables)


def on_device(records, fan_taps, dip_taps, live_mask, node_place, shot_place):
    _, comps, nodes, samples = records.shape
    taps = fan_taps.shape[1]
    reach = (taps - 1) // 2
    wide = 2 * reach
    devices = lax.axis_size("shot")
    group = nodes // devices

    block = records[0]
    count = lax.axis_size("tm")
    forward = [(i, i + 1) for i in range(count - 1)]
    backward = [(target, source) for source, target in forward]
    prev = lax.ppermute(block, "tm", forward)
    nxt = lax.ppermute(block, "tm", backward)
    place = lax.axis_index("tm")
    lane = jnp.arange(LANES, dtype=jnp.int32) % wide
    edge = jnp.where(lane < reach, place > 0, place < count - 1).astype(jnp.float32)[None, :]
    packed = fan_call(node_place[None, :], edge, live_mask, block, prev, nxt, circulant(fan_taps, samples))

    sent = packed.reshape(devices, group, packed.shape[-1])
    arrived = lax.all_to_all(sent, "shot", split_axis=0, concat_axis=0, tiled=True)
    data = arrived.reshape(devices * group, packed.shape[-1])
    target = (jnp.repeat(shot_place, group) * group + jnp.tile(jnp.arange(group, dtype=jnp.int32), devices))[None, :]
    out = dip_call(target, data, circulant(dip_taps[None], samples), group, comps)
    return out.reshape(comps, devices, group, samples).transpose(1, 0, 2, 3)


def solution(mesh):
    return jax.shard_map(
        on_device,
        mesh=mesh,
        in_specs=(P("shot", None, None, "tm"), P(), P(), P("shot", None), P(), P()),
        out_specs=P(None, None, "shot", "tm"),
        check_vma=False,
    )
```

```python
import functools

import jax
import jax.numpy as jnp
from jax import lax
from jax.experimental import pallas as pl
from jax.experimental.pallas import tpu as pltpu
from jax.sharding import PartitionSpec as P

LANES = 128
EXT = 256


def time_halo(block, axis, width):
    count = lax.axis_size(axis)
    forward = [(i, i + 1) for i in range(count - 1)]
    backward = [(target, source) for source, target in forward]
    samples = block.shape[-1]
    low = lax.ppermute(lax.slice_in_dim(block, samples - width, None, axis=-1), axis, forward)
    high = lax.ppermute(lax.slice_in_dim(block, 0, width, axis=-1), axis, backward)
    return low, high


def circulant(tap_set, samples):
    taps = tap_set.shape[-1]
    reach = (taps - 1) // 2
    j = jnp.arange(EXT, dtype=jnp.int32)
    t = jnp.arange(samples, dtype=jnp.int32)
    b = (j[:, None] - t[None, :] + reach) % EXT
    onehot = (b[:, :, None] == jnp.arange(taps, dtype=jnp.int32)[None, None, :]).astype(jnp.bfloat16)
    tables = jnp.einsum("gab,jtb->gajt", tap_set, onehot, preferred_element_type=jnp.float32)
    return tables.astype(jnp.bfloat16)


def fan_kernel(place_ref, edge_ref, ext_ref, table_ref, out_ref, scr_ref, halo_ref, *, taps, live_col, comps):
    c = pl.program_id(0)
    rows = ext_ref.shape[1]
    samples = LANES
    reach = (taps - 1) // 2
    place = place_ref[...]
    select = (lax.broadcasted_iota(jnp.int32, (rows, rows), 0) == place).astype(jnp.bfloat16)
    ordered = jnp.dot(select, ext_ref[0], preferred_element_type=jnp.float32)
    keep = ordered[:, live_col:live_col + 1]
    ordered = ordered.astype(jnp.bfloat16)
    swapped = jnp.concatenate([ordered[:, samples:], ordered[:, :samples]], axis=1)
    second = rows + 16
    zeros = jnp.zeros((8, LANES), jnp.float32)
    scr_ref[0:8, :] = zeros
    scr_ref[rows + 8:rows + 16, :] = zeros
    scr_ref[second + rows:second + rows + 8, :] = zeros
    acc = jnp.zeros((rows, LANES), jnp.float32)
    acc_h = jnp.zeros((rows, LANES), jnp.float32)
    for a in range(taps):
        table = table_ref[0, a]
        scr_ref[8:rows + 8, :] = jnp.dot(ordered, table, preferred_element_type=jnp.float32)
        scr_ref[second:second + rows, :] = jnp.dot(swapped, table, preferred_element_type=jnp.float32)
        acc = acc + scr_ref[pl.ds(a + 8 - reach, rows), :]
        acc_h = acc_h + scr_ref[pl.ds(second + a - reach, rows), :]
    out_ref[:, pl.ds(pl.multiple_of(c * samples, samples), samples)] = (acc * keep).astype(out_ref.dtype)
    lane = lax.broadcasted_iota(jnp.int32, (rows, LANES), 1)
    for k in range(comps):
        @pl.when(c == k)
        def _():
            moved = pltpu.roll(acc_h, reach + 2 * reach * k, 1)
            mine = jnp.where((lane >= 2 * reach * k) & (lane < 2 * reach * (k + 1)), moved, 0.0)
            if k == 0:
                halo_ref[...] = mine
            else:
                halo_ref[...] += mine

    @pl.when(c == comps - 1)
    def _():
        out_ref[:, comps * samples:(comps + 1) * samples] = (halo_ref[...] * keep * edge_ref[...]).astype(out_ref.dtype)


def dip_kernel(target_ref, data_ref, table_ref, out_ref, *, taps, group, comps):
    rows = data_ref.shape[0]
    samples = LANES
    reach = (taps - 1) // 2
    stride = comps * group
    out_rows = out_ref.shape[0]
    target = target_ref[...]
    row = lax.broadcasted_iota(jnp.int32, (out_rows, rows), 0)
    halo = data_ref[:, comps * samples:(comps + 1) * samples].astype(jnp.float32)
    selects, parts = [], []
    for c in range(comps):
        mine = pltpu.roll(halo, (samples - reach - 2 * reach * c) % samples, 1).astype(jnp.bfloat16)
        parts.append(jnp.concatenate([data_ref[:, c * samples:(c + 1) * samples], mine], axis=1))
        selects.append((row == target + group * c).astype(jnp.bfloat16))
    gathered = jnp.dot(jnp.concatenate(selects, axis=1), jnp.concatenate(parts, axis=0), preferred_element_type=jnp.float32)
    gathered = gathered.astype(jnp.bfloat16)
    acc = jnp.zeros((out_rows, LANES), jnp.float32)
    for a in range(taps):
        part = jnp.dot(gathered, table_ref[0, a], preferred_element_type=jnp.float32)
        shift = stride * (a - reach)
        if shift > 0:
            part = jnp.concatenate([part[shift:], jnp.zeros((shift, LANES), jnp.float32)], axis=0)
        elif shift < 0:
            part = jnp.concatenate([jnp.zeros((-shift, LANES), jnp.float32), part[:shift]], axis=0)
        acc = acc + part
    out_ref[...] = acc.astype(out_ref.dtype)


def fan_call(place, edge, ext, tables, live_col):
    comps, rows, _ = ext.shape
    taps = tables.shape[1]
    kernel = functools.partial(fan_kernel, taps=taps, live_col=live_col, comps=comps)
    return pl.pallas_call(
        kernel,
        grid=(comps,),
        in_specs=[
            pl.BlockSpec((1, rows), lambda c: (0, 0)),
            pl.BlockSpec((1, LANES), lambda c: (0, 0)),
            pl.BlockSpec((1, rows, EXT), lambda c: (c, 0, 0)),
            pl.BlockSpec((1, taps, EXT, LANES), lambda c: (c, 0, 0, 0)),
        ],
        out_specs=pl.BlockSpec((rows, (comps + 1) * LANES), lambda c: (0, 0)),
        out_shape=jax.ShapeDtypeStruct((rows, (comps + 1) * LANES), jnp.bfloat16),
        scratch_shapes=[pltpu.VMEM((2 * rows + 24, LANES), jnp.float32), pltpu.VMEM((rows, LANES), jnp.float32)],
    )(place, edge, ext, tables)


def dip_call(target, data, tables, group, comps):
    rows = data.shape[0]
    taps = tables.shape[1]
    kernel = functools.partial(dip_kernel, taps=taps, group=group, comps=comps)
    return pl.pallas_call(
        kernel,
        out_shape=jax.ShapeDtypeStruct((rows * comps, LANES), jnp.bfloat16),
    )(target, data, tables)


def on_device(records, fan_taps, dip_taps, live_mask, node_place, shot_place):
    _, comps, nodes, samples = records.shape
    taps = fan_taps.shape[1]
    reach = (taps - 1) // 2
    wide = 2 * reach
    devices = lax.axis_size("shot")
    group = nodes // devices

    block = records[0]
    low, high = time_halo(block, "tm", wide)
    live_col = samples + 32
    live = jnp.broadcast_to(live_mask[0].astype(jnp.bfloat16)[None, :, None], (comps, nodes, 1))
    gap1 = jnp.zeros((comps, nodes, live_col - samples - wide), jnp.bfloat16)
    gap2 = jnp.zeros((comps, nodes, EXT - wide - live_col - 1), jnp.bfloat16)
    ext = jnp.concatenate([block, high, gap1, live, gap2, low], axis=-1)
    place = lax.axis_index("tm")
    lane = jnp.arange(LANES, dtype=jnp.int32) % wide
    edge = jnp.where(lane < reach, place > 0, place < lax.axis_size("tm") - 1).astype(jnp.float32)[None, :]
    packed = fan_call(node_place[None, :], edge, ext, circulant(fan_taps, samples), live_col)

    sent = packed.reshape(devices, group, packed.shape[-1])
    arrived = lax.all_to_all(sent, "shot", split_axis=0, concat_axis=0, tiled=True)
    data = arrived.reshape(devices * group, packed.shape[-1])
    spread = comps * group
    target = (jnp.repeat(shot_place, group) * spread + jnp.tile(jnp.arange(group, dtype=jnp.int32), devices))[None, :]
    out = dip_call(target, data, circulant(dip_taps[None], samples), group, comps)
    return out.reshape(devices, comps, group, samples)


def solution(mesh):
    return jax.shard_map(
        on_device,
        mesh=mesh,
        in_specs=(P("shot", None, None, "tm"), P(), P(), P("shot", None), P(), P()),
        out_specs=P(None, None, "shot", "tm"),
        check_vma=False,
    )
```

```python
import functools

import jax
import jax.numpy as jnp
from jax import lax
from jax.experimental import pallas as pl
from jax.experimental.pallas import tpu as pltpu
from jax.sharding import PartitionSpec as P

LANES = 128
EXT = 256


def time_halo(block, axis, width):
    count = lax.axis_size(axis)
    forward = [(i, i + 1) for i in range(count - 1)]
    backward = [(target, source) for source, target in forward]
    samples = block.shape[-1]
    low = lax.ppermute(lax.slice_in_dim(block, samples - width, None, axis=-1), axis, forward)
    high = lax.ppermute(lax.slice_in_dim(block, 0, width, axis=-1), axis, backward)
    return low, high


def circulant(tap_set, samples):
    taps = tap_set.shape[-1]
    reach = (taps - 1) // 2
    j = jnp.arange(EXT, dtype=jnp.int32)
    t = jnp.arange(samples, dtype=jnp.int32)
    b = (j[:, None] - t[None, :] + reach) % EXT
    onehot = (b[:, :, None] == jnp.arange(taps, dtype=jnp.int32)[None, None, :]).astype(jnp.bfloat16)
    tables = jnp.einsum("gab,jtb->gajt", tap_set, onehot, preferred_element_type=jnp.float32)
    return tables.astype(jnp.bfloat16)


def fan_kernel(place_ref, edge_ref, live_ref, block_ref, prev_ref, next_ref, table_ref, out_ref, scr_ref, halo_ref, *, taps, comps):
    c = pl.program_id(0)
    rows = block_ref.shape[1]
    samples = LANES
    reach = (taps - 1) // 2
    wide = 2 * reach
    place = place_ref[...]
    select = (lax.broadcasted_iota(jnp.int32, (rows, rows), 0) == place).astype(jnp.bfloat16)
    keep = jnp.sum(select.astype(jnp.float32) * live_ref[...].astype(jnp.float32), axis=1, keepdims=True)
    lane = lax.broadcasted_iota(jnp.int32, (rows, LANES), 1)
    outer = jnp.where(lane < wide, next_ref[0], jnp.where(lane >= LANES - wide, prev_ref[0], jnp.zeros_like(prev_ref[0])))
    ext = jnp.concatenate([block_ref[0], outer], axis=1)
    ordered = jnp.dot(select, ext, preferred_element_type=jnp.float32).astype(jnp.bfloat16)
    swapped = jnp.concatenate([ordered[:, samples:], ordered[:, :samples]], axis=1)
    second = rows + 16
    zeros = jnp.zeros((8, LANES), jnp.float32)
    scr_ref[0:8, :] = zeros
    scr_ref[rows + 8:rows + 16, :] = zeros
    scr_ref[second + rows:second + rows + 8, :] = zeros
    acc = jnp.zeros((rows, LANES), jnp.float32)
    acc_h = jnp.zeros((rows, LANES), jnp.float32)
    for a in range(taps):
        table = table_ref[0, a]
        scr_ref[8:rows + 8, :] = jnp.dot(ordered, table, preferred_element_type=jnp.float32)
        scr_ref[second:second + rows, :] = jnp.dot(swapped, table, preferred_element_type=jnp.float32)
        acc = acc + scr_ref[pl.ds(a + 8 - reach, rows), :]
        acc_h = acc_h + scr_ref[pl.ds(second + a - reach, rows), :]
    out_ref[:, pl.ds(pl.multiple_of(c * samples, samples), samples)] = (acc * keep).astype(out_ref.dtype)
    for k in range(comps):
        @pl.when(c == k)
        def _():
            moved = pltpu.roll(acc_h, reach + 2 * reach * k, 1)
            mine = jnp.where((lane >= 2 * reach * k) & (lane < 2 * reach * (k + 1)), moved, 0.0)
            if k == 0:
                halo_ref[...] = mine
            else:
                halo_ref[...] += mine

    @pl.when(c == comps - 1)
    def _():
        out_ref[:, comps * samples:(comps + 1) * samples] = (halo_ref[...] * keep * edge_ref[...]).astype(out_ref.dtype)


def dip_kernel(target_ref, data_ref, table_ref, out_ref, *, taps, group, comps):
    rows = data_ref.shape[0]
    samples = LANES
    reach = (taps - 1) // 2
    stride = comps * group
    out_rows = out_ref.shape[0]
    target = target_ref[...]
    row = lax.broadcasted_iota(jnp.int32, (out_rows, rows), 0)
    halo = data_ref[:, comps * samples:(comps + 1) * samples].astype(jnp.float32)
    selects, parts = [], []
    for c in range(comps):
        mine = pltpu.roll(halo, (samples - reach - 2 * reach * c) % samples, 1).astype(jnp.bfloat16)
        parts.append(jnp.concatenate([data_ref[:, c * samples:(c + 1) * samples], mine], axis=1))
        selects.append((row == target + group * c).astype(jnp.bfloat16))
    gathered = jnp.dot(jnp.concatenate(selects, axis=1), jnp.concatenate(parts, axis=0), preferred_element_type=jnp.float32)
    gathered = gathered.astype(jnp.bfloat16)
    acc = jnp.zeros((out_rows, LANES), jnp.float32)
    for a in range(taps):
        part = jnp.dot(gathered, table_ref[0, a], preferred_element_type=jnp.float32)
        shift = stride * (a - reach)
        if shift > 0:
            part = jnp.concatenate([part[shift:], jnp.zeros((shift, LANES), jnp.float32)], axis=0)
        elif shift < 0:
            part = jnp.concatenate([jnp.zeros((-shift, LANES), jnp.float32), part[:shift]], axis=0)
        acc = acc + part
    out_ref[...] = acc.astype(out_ref.dtype)


def fan_call(place, edge, live, block, prev, nxt, tables):
    comps, rows, samples = block.shape
    taps = tables.shape[1]
    kernel = functools.partial(fan_kernel, taps=taps, comps=comps)
    part = pl.BlockSpec((1, rows, samples), lambda c: (c, 0, 0))
    return pl.pallas_call(
        kernel,
        grid=(comps,),
        in_specs=[
            pl.BlockSpec((1, rows), lambda c: (0, 0)),
            pl.BlockSpec((1, LANES), lambda c: (0, 0)),
            pl.BlockSpec((1, rows), lambda c: (0, 0)),
            part,
            part,
            part,
            pl.BlockSpec((1, taps, EXT, LANES), lambda c: (c, 0, 0, 0)),
        ],
        out_specs=pl.BlockSpec((rows, (comps + 1) * LANES), lambda c: (0, 0)),
        out_shape=jax.ShapeDtypeStruct((rows, (comps + 1) * LANES), jnp.bfloat16),
        scratch_shapes=[pltpu.VMEM((2 * rows + 24, LANES), jnp.float32), pltpu.VMEM((rows, LANES), jnp.float32)],
    )(place, edge, live, block, prev, nxt, tables)


def dip_call(target, data, tables, group, comps):
    rows = data.shape[0]
    taps = tables.shape[1]
    kernel = functools.partial(dip_kernel, taps=taps, group=group, comps=comps)
    return pl.pallas_call(
        kernel,
        out_shape=jax.ShapeDtypeStruct((rows * comps, LANES), jnp.bfloat16),
    )(target, data, tables)


def on_device(records, fan_taps, dip_taps, live_mask, node_place, shot_place):
    _, comps, nodes, samples = records.shape
    taps = fan_taps.shape[1]
    reach = (taps - 1) // 2
    wide = 2 * reach
    devices = lax.axis_size("shot")
    group = nodes // devices

    block = records[0]
    count = lax.axis_size("tm")
    forward = [(i, i + 1) for i in range(count - 1)]
    backward = [(target, source) for source, target in forward]
    prev = lax.ppermute(block, "tm", forward)
    nxt = lax.ppermute(block, "tm", backward)
    place = lax.axis_index("tm")
    lane = jnp.arange(LANES, dtype=jnp.int32) % wide
    edge = jnp.where(lane < reach, place > 0, place < count - 1).astype(jnp.float32)[None, :]
    packed = fan_call(node_place[None, :], edge, live_mask, block, prev, nxt, circulant(fan_taps, samples))

    sent = packed.reshape(devices, group, packed.shape[-1])
    arrived = lax.all_to_all(sent, "shot", split_axis=0, concat_axis=0, tiled=True)
    data = arrived.reshape(devices * group, packed.shape[-1])
    spread = comps * group
    target = (jnp.repeat(shot_place, group) * spread + jnp.tile(jnp.arange(group, dtype=jnp.int32), devices))[None, :]
    out = dip_call(target, data, circulant(dip_taps[None], samples), group, comps)
    return out.reshape(devices, comps, group, samples)


def solution(mesh):
    return jax.shard_map(
        on_device,
        mesh=mesh,
        in_specs=(P("shot", None, None, "tm"), P(), P(), P("shot", None), P(), P()),
        out_specs=P(None, None, "shot", "tm"),
        check_vma=False,
    )
```

```python
import functools

import jax
import jax.numpy as jnp
from jax import lax
from jax.experimental import pallas as pl
from jax.experimental.pallas import tpu as pltpu
from jax.sharding import PartitionSpec as P

LANES = 128
EXT = 256


def time_halo(block, axis, width):
    count = lax.axis_size(axis)
    forward = [(i, i + 1) for i in range(count - 1)]
    backward = [(target, source) for source, target in forward]
    samples = block.shape[-1]
    low = lax.ppermute(lax.slice_in_dim(block, samples - width, None, axis=-1), axis, forward)
    high = lax.ppermute(lax.slice_in_dim(block, 0, width, axis=-1), axis, backward)
    return low, high


def circulant(tap_set, samples):
    taps = tap_set.shape[-1]
    reach = (taps - 1) // 2
    j = jnp.arange(EXT, dtype=jnp.int32)
    t = jnp.arange(samples, dtype=jnp.int32)
    b = (j[:, None] - t[None, :] + reach) % EXT
    onehot = (b[:, :, None] == jnp.arange(taps, dtype=jnp.int32)[None, None, :]).astype(jnp.bfloat16)
    tables = jnp.einsum("gab,jtb->gajt", tap_set, onehot, preferred_element_type=jnp.float32)
    return tables.astype(jnp.bfloat16)


def fan_kernel(place_ref, edge_ref, ext_ref, table_ref, out_ref, scr_ref, halo_ref, *, taps, live_col, comps):
    c = pl.program_id(0)
    rows = ext_ref.shape[1]
    samples = LANES
    reach = (taps - 1) // 2
    place = place_ref[...]
    select = (lax.broadcasted_iota(jnp.int32, (rows, rows), 0) == place).astype(jnp.bfloat16)
    ordered = jnp.dot(select, ext_ref[0], preferred_element_type=jnp.float32)
    keep = ordered[:, live_col:live_col + 1]
    zeros = jnp.zeros((8, EXT), jnp.float32)
    scr_ref[0:8, :] = zeros
    scr_ref[rows + 8:rows + 16, :] = zeros
    scr_ref[8:rows + 8, :] = ordered
    acc = jnp.zeros((rows, LANES), jnp.float32)
    acc_h = jnp.zeros((rows, LANES), jnp.float32)
    for a in range(taps):
        table = table_ref[0, a]
        moved = scr_ref[pl.ds(a + 8 - reach, rows), :].astype(jnp.bfloat16)
        swapped = jnp.concatenate([moved[:, samples:], moved[:, :samples]], axis=1)
        acc = acc + jnp.dot(moved, table, preferred_element_type=jnp.float32)
        acc_h = acc_h + jnp.dot(swapped, table, preferred_element_type=jnp.float32)
    out_ref[:, pl.ds(pl.multiple_of(c * samples, samples), samples)] = (acc * keep).astype(out_ref.dtype)
    lane = lax.broadcasted_iota(jnp.int32, (rows, LANES), 1)
    for k in range(comps):
        @pl.when(c == k)
        def _():
            moved = pltpu.roll(acc_h, reach + 2 * reach * k, 1)
            mine = jnp.where((lane >= 2 * reach * k) & (lane < 2 * reach * (k + 1)), moved, 0.0)
            if k == 0:
                halo_ref[...] = mine
            else:
                halo_ref[...] += mine

    @pl.when(c == comps - 1)
    def _():
        out_ref[:, comps * samples:(comps + 1) * samples] = (halo_ref[...] * keep * edge_ref[...]).astype(out_ref.dtype)


def dip_kernel(target_ref, data_ref, table_ref, out_ref, *, taps, group, comps):
    rows = data_ref.shape[0]
    samples = LANES
    reach = (taps - 1) // 2
    stride = comps * group
    out_rows = out_ref.shape[0]
    target = target_ref[...]
    row = lax.broadcasted_iota(jnp.int32, (out_rows, rows), 0)
    halo = data_ref[:, comps * samples:(comps + 1) * samples].astype(jnp.float32)
    selects, parts = [], []
    for c in range(comps):
        mine = pltpu.roll(halo, (samples - reach - 2 * reach * c) % samples, 1).astype(jnp.bfloat16)
        parts.append(jnp.concatenate([data_ref[:, c * samples:(c + 1) * samples], mine], axis=1))
        selects.append((row == target + group * c).astype(jnp.bfloat16))
    gathered = jnp.dot(jnp.concatenate(selects, axis=1), jnp.concatenate(parts, axis=0), preferred_element_type=jnp.float32)
    gathered = gathered.astype(jnp.bfloat16)
    acc = jnp.zeros((out_rows, LANES), jnp.float32)
    for a in range(taps):
        part = jnp.dot(gathered, table_ref[0, a], preferred_element_type=jnp.float32)
        shift = stride * (a - reach)
        if shift > 0:
            part = jnp.concatenate([part[shift:], jnp.zeros((shift, LANES), jnp.float32)], axis=0)
        elif shift < 0:
            part = jnp.concatenate([jnp.zeros((-shift, LANES), jnp.float32), part[:shift]], axis=0)
        acc = acc + part
    out_ref[...] = acc.astype(out_ref.dtype)


def fan_call(place, edge, ext, tables, live_col):
    comps, rows, _ = ext.shape
    taps = tables.shape[1]
    kernel = functools.partial(fan_kernel, taps=taps, live_col=live_col, comps=comps)
    return pl.pallas_call(
        kernel,
        grid=(comps,),
        in_specs=[
            pl.BlockSpec((1, rows), lambda c: (0, 0)),
            pl.BlockSpec((1, LANES), lambda c: (0, 0)),
            pl.BlockSpec((1, rows, EXT), lambda c: (c, 0, 0)),
            pl.BlockSpec((1, taps, EXT, LANES), lambda c: (c, 0, 0, 0)),
        ],
        out_specs=pl.BlockSpec((rows, (comps + 1) * LANES), lambda c: (0, 0)),
        out_shape=jax.ShapeDtypeStruct((rows, (comps + 1) * LANES), jnp.bfloat16),
        scratch_shapes=[pltpu.VMEM((rows + 16, EXT), jnp.float32), pltpu.VMEM((rows, LANES), jnp.float32)],
    )(place, edge, ext, tables)


def dip_call(target, data, tables, group, comps):
    rows = data.shape[0]
    taps = tables.shape[1]
    kernel = functools.partial(dip_kernel, taps=taps, group=group, comps=comps)
    return pl.pallas_call(
        kernel,
        out_shape=jax.ShapeDtypeStruct((rows * comps, LANES), jnp.bfloat16),
    )(target, data, tables)


def on_device(records, fan_taps, dip_taps, live_mask, node_place, shot_place):
    _, comps, nodes, samples = records.shape
    taps = fan_taps.shape[1]
    reach = (taps - 1) // 2
    wide = 2 * reach
    devices = lax.axis_size("shot")
    group = nodes // devices

    block = records[0]
    low, high = time_halo(block, "tm", wide)
    live_col = samples + 32
    live = jnp.broadcast_to(live_mask[0].astype(jnp.bfloat16)[None, :, None], (comps, nodes, 1))
    gap1 = jnp.zeros((comps, nodes, live_col - samples - wide), jnp.bfloat16)
    gap2 = jnp.zeros((comps, nodes, EXT - wide - live_col - 1), jnp.bfloat16)
    ext = jnp.concatenate([block, high, gap1, live, gap2, low], axis=-1)
    place = lax.axis_index("tm")
    lane = jnp.arange(LANES, dtype=jnp.int32) % wide
    edge = jnp.where(lane < reach, place > 0, place < lax.axis_size("tm") - 1).astype(jnp.float32)[None, :]
    packed = fan_call(node_place[None, :], edge, ext, circulant(fan_taps, samples), live_col)

    sent = packed.reshape(devices, group, packed.shape[-1])
    arrived = lax.all_to_all(sent, "shot", split_axis=0, concat_axis=0, tiled=True)
    data = arrived.reshape(devices * group, packed.shape[-1])
    spread = comps * group
    target = (jnp.repeat(shot_place, group) * spread + jnp.tile(jnp.arange(group, dtype=jnp.int32), devices))[None, :]
    out = dip_call(target, data, circulant(dip_taps[None], samples), group, comps)
    return out.reshape(devices, comps, group, samples)


def solution(mesh):
    return jax.shard_map(
        on_device,
        mesh=mesh,
        in_specs=(P("shot", None, None, "tm"), P(), P(), P("shot", None), P(), P()),
        out_specs=P(None, None, "shot", "tm"),
        check_vma=False,
    )
```

```python
import functools

import jax
import jax.numpy as jnp
from jax import lax
from jax.experimental import pallas as pl
from jax.experimental.pallas import tpu as pltpu
from jax.sharding import PartitionSpec as P

LANES = 128
EXT = 256


def time_halo(block, axis, width):
    count = lax.axis_size(axis)
    forward = [(i, i + 1) for i in range(count - 1)]
    backward = [(target, source) for source, target in forward]
    samples = block.shape[-1]
    low = lax.ppermute(lax.slice_in_dim(block, samples - width, None, axis=-1), axis, forward)
    high = lax.ppermute(lax.slice_in_dim(block, 0, width, axis=-1), axis, backward)
    return low, high


def circulant(tap_set, samples):
    taps = tap_set.shape[-1]
    reach = (taps - 1) // 2
    j = jnp.arange(EXT, dtype=jnp.int32)
    t = jnp.arange(samples, dtype=jnp.int32)
    b = (j[:, None] - t[None, :] + reach) % EXT
    onehot = (b[:, :, None] == jnp.arange(taps, dtype=jnp.int32)[None, None, :]).astype(jnp.bfloat16)
    tables = jnp.einsum("gab,jtb->gajt", tap_set, onehot, preferred_element_type=jnp.float32)
    return tables.astype(jnp.bfloat16)


def fan_kernel(place_ref, edge_ref, ext_ref, table_ref, out_ref, scr_ref, halo_ref, *, taps, live_col, comps):
    c = pl.program_id(0)
    rows = ext_ref.shape[1]
    samples = LANES
    reach = (taps - 1) // 2
    place = place_ref[...]
    select = (lax.broadcasted_iota(jnp.int32, (rows, rows), 0) == place).astype(jnp.bfloat16)
    ordered = jnp.dot(select, ext_ref[0], preferred_element_type=jnp.float32)
    keep = ordered[:, live_col:live_col + 1]
    zeros = jnp.zeros((8, EXT), jnp.float32)
    scr_ref[0:8, :] = zeros
    scr_ref[rows + 8:rows + 16, :] = zeros
    scr_ref[8:rows + 8, :] = ordered
    acc = jnp.zeros((rows, LANES), jnp.float32)
    acc_h = jnp.zeros((rows, LANES), jnp.float32)
    for a in range(taps):
        table = table_ref[0, a]
        both = jnp.concatenate([table, jnp.concatenate([table[samples:], table[:samples]], axis=0)], axis=1)
        moved = scr_ref[pl.ds(a + 8 - reach, rows), :].astype(jnp.bfloat16)
        part = jnp.dot(moved, both, preferred_element_type=jnp.float32)
        acc = acc + part[:, :samples]
        acc_h = acc_h + part[:, samples:]
    out_ref[:, pl.ds(pl.multiple_of(c * samples, samples), samples)] = (acc * keep).astype(out_ref.dtype)
    lane = lax.broadcasted_iota(jnp.int32, (rows, LANES), 1)
    for k in range(comps):
        @pl.when(c == k)
        def _():
            moved = pltpu.roll(acc_h, reach + 2 * reach * k, 1)
            mine = jnp.where((lane >= 2 * reach * k) & (lane < 2 * reach * (k + 1)), moved, 0.0)
            if k == 0:
                halo_ref[...] = mine
            else:
                halo_ref[...] += mine

    @pl.when(c == comps - 1)
    def _():
        out_ref[:, comps * samples:(comps + 1) * samples] = (halo_ref[...] * keep * edge_ref[...]).astype(out_ref.dtype)


def dip_kernel(target_ref, data_ref, table_ref, out_ref, *, taps, group, comps):
    rows = data_ref.shape[0]
    samples = LANES
    reach = (taps - 1) // 2
    stride = comps * group
    out_rows = out_ref.shape[0]
    target = target_ref[...]
    row = lax.broadcasted_iota(jnp.int32, (out_rows, rows), 0)
    halo = data_ref[:, comps * samples:(comps + 1) * samples].astype(jnp.float32)
    selects, parts = [], []
    for c in range(comps):
        mine = pltpu.roll(halo, (samples - reach - 2 * reach * c) % samples, 1).astype(jnp.bfloat16)
        parts.append(jnp.concatenate([data_ref[:, c * samples:(c + 1) * samples], mine], axis=1))
        selects.append((row == target + group * c).astype(jnp.bfloat16))
    gathered = jnp.dot(jnp.concatenate(selects, axis=1), jnp.concatenate(parts, axis=0), preferred_element_type=jnp.float32)
    gathered = gathered.astype(jnp.bfloat16)
    acc = jnp.zeros((out_rows, LANES), jnp.float32)
    for first in range(0, taps, 2):
        pair = list(range(first, min(first + 2, taps)))
        tables = jnp.concatenate([table_ref[0, a] for a in pair], axis=1)
        both = jnp.dot(gathered, tables, preferred_element_type=jnp.float32)
        for k, a in enumerate(pair):
            part = both[:, k * samples:(k + 1) * samples]
            shift = stride * (a - reach)
            if shift > 0:
                part = jnp.concatenate([part[shift:], jnp.zeros((shift, LANES), jnp.float32)], axis=0)
            elif shift < 0:
                part = jnp.concatenate([jnp.zeros((-shift, LANES), jnp.float32), part[:shift]], axis=0)
            acc = acc + part
    out_ref[...] = acc.astype(out_ref.dtype)


def fan_call(place, edge, ext, tables, live_col):
    comps, rows, _ = ext.shape
    taps = tables.shape[1]
    kernel = functools.partial(fan_kernel, taps=taps, live_col=live_col, comps=comps)
    return pl.pallas_call(
        kernel,
        grid=(comps,),
        in_specs=[
            pl.BlockSpec((1, rows), lambda c: (0, 0)),
            pl.BlockSpec((1, LANES), lambda c: (0, 0)),
            pl.BlockSpec((1, rows, EXT), lambda c: (c, 0, 0)),
            pl.BlockSpec((1, taps, EXT, LANES), lambda c: (c, 0, 0, 0)),
        ],
        out_specs=pl.BlockSpec((rows, (comps + 1) * LANES), lambda c: (0, 0)),
        out_shape=jax.ShapeDtypeStruct((rows, (comps + 1) * LANES), jnp.bfloat16),
        scratch_shapes=[pltpu.VMEM((rows + 16, EXT), jnp.float32), pltpu.VMEM((rows, LANES), jnp.float32)],
    )(place, edge, ext, tables)


def dip_call(target, data, tables, group, comps):
    rows = data.shape[0]
    taps = tables.shape[1]
    kernel = functools.partial(dip_kernel, taps=taps, group=group, comps=comps)
    return pl.pallas_call(
        kernel,
        out_shape=jax.ShapeDtypeStruct((rows * comps, LANES), jnp.bfloat16),
    )(target, data, tables)


def on_device(records, fan_taps, dip_taps, live_mask, node_place, shot_place):
    _, comps, nodes, samples = records.shape
    taps = fan_taps.shape[1]
    reach = (taps - 1) // 2
    wide = 2 * reach
    devices = lax.axis_size("shot")
    group = nodes // devices

    block = records[0]
    low, high = time_halo(block, "tm", wide)
    live_col = samples + 32
    live = jnp.broadcast_to(live_mask[0].astype(jnp.bfloat16)[None, :, None], (comps, nodes, 1))
    gap1 = jnp.zeros((comps, nodes, live_col - samples - wide), jnp.bfloat16)
    gap2 = jnp.zeros((comps, nodes, EXT - wide - live_col - 1), jnp.bfloat16)
    ext = jnp.concatenate([block, high, gap1, live, gap2, low], axis=-1)
    place = lax.axis_index("tm")
    lane = jnp.arange(LANES, dtype=jnp.int32) % wide
    edge = jnp.where(lane < reach, place > 0, place < lax.axis_size("tm") - 1).astype(jnp.float32)[None, :]
    packed = fan_call(node_place[None, :], edge, ext, circulant(fan_taps, samples), live_col)

    sent = packed.reshape(devices, group, packed.shape[-1])
    arrived = lax.all_to_all(sent, "shot", split_axis=0, concat_axis=0, tiled=True)
    data = arrived.reshape(devices * group, packed.shape[-1])
    spread = comps * group
    target = (jnp.repeat(shot_place, group) * spread + jnp.tile(jnp.arange(group, dtype=jnp.int32), devices))[None, :]
    out = dip_call(target, data, circulant(dip_taps[None], samples), group, comps)
    return out.reshape(devices, comps, group, samples)


def solution(mesh):
    return jax.shard_map(
        on_device,
        mesh=mesh,
        in_specs=(P("shot", None, None, "tm"), P(), P(), P("shot", None), P(), P()),
        out_specs=P(None, None, "shot", "tm"),
        check_vma=False,
    )
```

```python
import functools

import jax
import jax.numpy as jnp
from jax import lax
from jax.experimental import pallas as pl
from jax.experimental.pallas import tpu as pltpu
from jax.sharding import PartitionSpec as P

LANES = 128
EXT = 256


def time_halo(block, axis, width):
    count = lax.axis_size(axis)
    forward = [(i, i + 1) for i in range(count - 1)]
    backward = [(target, source) for source, target in forward]
    samples = block.shape[-1]
    low = lax.ppermute(lax.slice_in_dim(block, samples - width, None, axis=-1), axis, forward)
    high = lax.ppermute(lax.slice_in_dim(block, 0, width, axis=-1), axis, backward)
    return low, high


def circulant(tap_set, samples):
    taps = tap_set.shape[-1]
    reach = (taps - 1) // 2
    j = jnp.arange(EXT, dtype=jnp.int32)
    t = jnp.arange(samples, dtype=jnp.int32)
    b = (j[:, None] - t[None, :] + reach) % EXT
    onehot = (b[:, :, None] == jnp.arange(taps, dtype=jnp.int32)[None, None, :]).astype(jnp.bfloat16)
    tables = jnp.einsum("gab,jtb->gajt", tap_set, onehot, preferred_element_type=jnp.float32)
    return tables.astype(jnp.bfloat16)


def fan_kernel(place_ref, edge_ref, ext_ref, table_ref, out_ref, scr_ref, halo_ref, *, taps, live_col, comps):
    c = pl.program_id(0)
    rows = ext_ref.shape[1]
    samples = LANES
    reach = (taps - 1) // 2
    place = place_ref[...]
    select = (lax.broadcasted_iota(jnp.int32, (rows, rows), 0) == place).astype(jnp.bfloat16)
    ordered = jnp.dot(select, ext_ref[0], preferred_element_type=jnp.float32)
    keep = ordered[:, live_col:live_col + 1]
    zeros = jnp.zeros((8, EXT), jnp.float32)
    scr_ref[0:8, :] = zeros
    scr_ref[rows + 8:rows + 16, :] = zeros
    scr_ref[8:rows + 8, :] = ordered
    acc = jnp.zeros((rows, LANES), jnp.float32)
    acc_h = jnp.zeros((rows, LANES), jnp.float32)
    for a in range(taps):
        table = table_ref[0, a]
        both = jnp.concatenate([table, jnp.concatenate([table[samples:], table[:samples]], axis=0)], axis=1)
        moved = scr_ref[pl.ds(a + 8 - reach, rows), :].astype(jnp.bfloat16)
        part = jnp.dot(moved, both, preferred_element_type=jnp.float32)
        acc = acc + part[:, :samples]
        acc_h = acc_h + part[:, samples:]
    out_ref[:, :, pl.ds(pl.multiple_of(c * samples, samples), samples)] = (acc * keep).astype(out_ref.dtype).reshape(rows // 2, 2, samples)
    lane = lax.broadcasted_iota(jnp.int32, (rows, LANES), 1)
    for k in range(comps):
        @pl.when(c == k)
        def _():
            moved = pltpu.roll(acc_h, reach + 2 * reach * k, 1)
            mine = jnp.where((lane >= 2 * reach * k) & (lane < 2 * reach * (k + 1)), moved, 0.0)
            if k == 0:
                halo_ref[...] = mine
            else:
                halo_ref[...] += mine

    @pl.when(c == comps - 1)
    def _():
        out_ref[:, :, comps * samples:(comps + 1) * samples] = (halo_ref[...] * keep * edge_ref[...]).astype(out_ref.dtype).reshape(rows // 2, 2, samples)


def dip_kernel(target_ref, data_ref, table_ref, out_ref, *, taps, group, comps):
    rows = data_ref.shape[0] * data_ref.shape[1]
    samples = LANES
    reach = (taps - 1) // 2
    stride = comps * group
    out_rows = out_ref.shape[0]
    target = target_ref[...]
    row = lax.broadcasted_iota(jnp.int32, (out_rows, rows), 0)
    halo = data_ref[:, :, comps * samples:(comps + 1) * samples].reshape(rows, samples).astype(jnp.float32)
    selects, parts = [], []
    for c in range(comps):
        mine = pltpu.roll(halo, (samples - reach - 2 * reach * c) % samples, 1).astype(jnp.bfloat16)
        parts.append(jnp.concatenate([data_ref[:, :, c * samples:(c + 1) * samples].reshape(rows, samples), mine], axis=1))
        selects.append((row == target + group * c).astype(jnp.bfloat16))
    gathered = jnp.dot(jnp.concatenate(selects, axis=1), jnp.concatenate(parts, axis=0), preferred_element_type=jnp.float32)
    gathered = gathered.astype(jnp.bfloat16)
    acc = jnp.zeros((out_rows, LANES), jnp.float32)
    for first in range(0, taps, 2):
        pair = list(range(first, min(first + 2, taps)))
        tables = jnp.concatenate([table_ref[0, a] for a in pair], axis=1)
        both = jnp.dot(gathered, tables, preferred_element_type=jnp.float32)
        for k, a in enumerate(pair):
            part = both[:, k * samples:(k + 1) * samples]
            shift = stride * (a - reach)
            if shift > 0:
                part = jnp.concatenate([part[shift:], jnp.zeros((shift, LANES), jnp.float32)], axis=0)
            elif shift < 0:
                part = jnp.concatenate([jnp.zeros((-shift, LANES), jnp.float32), part[:shift]], axis=0)
            acc = acc + part
    out_ref[...] = acc.astype(out_ref.dtype)


def fan_call(place, edge, ext, tables, live_col):
    comps, rows, _ = ext.shape
    taps = tables.shape[1]
    kernel = functools.partial(fan_kernel, taps=taps, live_col=live_col, comps=comps)
    return pl.pallas_call(
        kernel,
        grid=(comps,),
        in_specs=[
            pl.BlockSpec((1, rows), lambda c: (0, 0)),
            pl.BlockSpec((1, LANES), lambda c: (0, 0)),
            pl.BlockSpec((1, rows, EXT), lambda c: (c, 0, 0)),
            pl.BlockSpec((1, taps, EXT, LANES), lambda c: (c, 0, 0, 0)),
        ],
        out_specs=pl.BlockSpec((rows // 2, 2, (comps + 1) * LANES), lambda c: (0, 0, 0)),
        out_shape=jax.ShapeDtypeStruct((rows // 2, 2, (comps + 1) * LANES), jnp.bfloat16),
        scratch_shapes=[pltpu.VMEM((rows + 16, EXT), jnp.float32), pltpu.VMEM((rows, LANES), jnp.float32)],
    )(place, edge, ext, tables)


def dip_call(target, data, tables, group, comps):
    rows = data.shape[0] * data.shape[1]
    taps = tables.shape[1]
    kernel = functools.partial(dip_kernel, taps=taps, group=group, comps=comps)
    return pl.pallas_call(
        kernel,
        out_shape=jax.ShapeDtypeStruct((rows * comps, LANES), jnp.bfloat16),
    )(target, data, tables)


def on_device(records, fan_taps, dip_taps, live_mask, node_place, shot_place):
    _, comps, nodes, samples = records.shape
    taps = fan_taps.shape[1]
    reach = (taps - 1) // 2
    wide = 2 * reach
    devices = lax.axis_size("shot")
    group = nodes // devices

    block = records[0]
    low, high = time_halo(block, "tm", wide)
    live_col = samples + 32
    live = jnp.broadcast_to(live_mask[0].astype(jnp.bfloat16)[None, :, None], (comps, nodes, 1))
    gap1 = jnp.zeros((comps, nodes, live_col - samples - wide), jnp.bfloat16)
    gap2 = jnp.zeros((comps, nodes, EXT - wide - live_col - 1), jnp.bfloat16)
    ext = jnp.concatenate([block, high, gap1, live, gap2, low], axis=-1)
    place = lax.axis_index("tm")
    lane = jnp.arange(LANES, dtype=jnp.int32) % wide
    edge = jnp.where(lane < reach, place > 0, place < lax.axis_size("tm") - 1).astype(jnp.float32)[None, :]
    packed = fan_call(node_place[None, :], edge, ext, circulant(fan_taps, samples), live_col)

    data = lax.all_to_all(packed, "shot", split_axis=0, concat_axis=0, tiled=True)
    spread = comps * group
    target = (jnp.repeat(shot_place, group) * spread + jnp.tile(jnp.arange(group, dtype=jnp.int32), devices))[None, :]
    out = dip_call(target, data, circulant(dip_taps[None], samples), group, comps)
    return out.reshape(devices, comps, group, samples)


def solution(mesh):
    return jax.shard_map(
        on_device,
        mesh=mesh,
        in_specs=(P("shot", None, None, "tm"), P(), P(), P("shot", None), P(), P()),
        out_specs=P(None, None, "shot", "tm"),
        check_vma=False,
    )
```

```python
import functools

import jax
import jax.numpy as jnp
from jax import lax
from jax.experimental import pallas as pl
from jax.experimental.pallas import tpu as pltpu
from jax.sharding import PartitionSpec as P

LANES = 128
EXT = 256


def time_halo(block, axis, width):
    count = lax.axis_size(axis)
    forward = [(i, i + 1) for i in range(count - 1)]
    backward = [(target, source) for source, target in forward]
    samples = block.shape[-1]
    low = lax.ppermute(lax.slice_in_dim(block, samples - width, None, axis=-1), axis, forward)
    high = lax.ppermute(lax.slice_in_dim(block, 0, width, axis=-1), axis, backward)
    return low, high


def circulant(tap_set, samples):
    taps = tap_set.shape[-1]
    reach = (taps - 1) // 2
    j = jnp.arange(EXT, dtype=jnp.int32)
    t = jnp.arange(samples, dtype=jnp.int32)
    b = (j[:, None] - t[None, :] + reach) % EXT
    onehot = (b[:, :, None] == jnp.arange(taps, dtype=jnp.int32)[None, None, :]).astype(jnp.bfloat16)
    tables = jnp.einsum("gab,jtb->gajt", tap_set, onehot, preferred_element_type=jnp.float32)
    return tables.astype(jnp.bfloat16)


def fan_kernel(place_ref, edge_ref, live_ref, block_ref, prev_ref, next_ref, table_ref, out_ref, scr_ref, halo_ref, *, taps, comps):
    c = pl.program_id(0)
    rows = block_ref.shape[1]
    samples = LANES
    reach = (taps - 1) // 2
    wide = 2 * reach
    place = place_ref[...]
    select = (lax.broadcasted_iota(jnp.int32, (rows, rows), 0) == place).astype(jnp.bfloat16)
    keep = jnp.sum(select.astype(jnp.float32) * live_ref[...].astype(jnp.float32), axis=1, keepdims=True)
    lane = lax.broadcasted_iota(jnp.int32, (rows, LANES), 1)
    outer = jnp.where(lane < wide, next_ref[0], jnp.where(lane >= LANES - wide, prev_ref[0], jnp.zeros_like(prev_ref[0])))
    ext = jnp.concatenate([block_ref[0], outer], axis=1)
    ordered = jnp.dot(select, ext, preferred_element_type=jnp.float32)
    zeros = jnp.zeros((8, EXT), jnp.float32)
    scr_ref[0:8, :] = zeros
    scr_ref[rows + 8:rows + 16, :] = zeros
    scr_ref[8:rows + 8, :] = ordered
    acc = jnp.zeros((rows, LANES), jnp.float32)
    acc_h = jnp.zeros((rows, LANES), jnp.float32)
    for a in range(taps):
        table = table_ref[0, a]
        both = jnp.concatenate([table, jnp.concatenate([table[samples:], table[:samples]], axis=0)], axis=1)
        moved = scr_ref[pl.ds(a + 8 - reach, rows), :].astype(jnp.bfloat16)
        part = jnp.dot(moved, both, preferred_element_type=jnp.float32)
        acc = acc + part[:, :samples]
        acc_h = acc_h + part[:, samples:]
    out_ref[:, :, pl.ds(pl.multiple_of(c * samples, samples), samples)] = (acc * keep).astype(out_ref.dtype).reshape(rows // 2, 2, samples)
    for k in range(comps):
        @pl.when(c == k)
        def _():
            moved = pltpu.roll(acc_h, reach + 2 * reach * k, 1)
            mine = jnp.where((lane >= 2 * reach * k) & (lane < 2 * reach * (k + 1)), moved, 0.0)
            if k == 0:
                halo_ref[...] = mine
            else:
                halo_ref[...] += mine

    @pl.when(c == comps - 1)
    def _():
        out_ref[:, :, comps * samples:(comps + 1) * samples] = (halo_ref[...] * keep * edge_ref[...]).astype(out_ref.dtype).reshape(rows // 2, 2, samples)


def dip_kernel(target_ref, data_ref, table_ref, out_ref, *, taps, group, comps):
    rows = data_ref.shape[0] * data_ref.shape[1]
    samples = LANES
    reach = (taps - 1) // 2
    stride = comps * group
    out_rows = out_ref.shape[0]
    target = target_ref[...]
    row = lax.broadcasted_iota(jnp.int32, (out_rows, rows), 0)
    halo = data_ref[:, :, comps * samples:(comps + 1) * samples].reshape(rows, samples).astype(jnp.float32)
    selects, parts = [], []
    for c in range(comps):
        mine = pltpu.roll(halo, (samples - reach - 2 * reach * c) % samples, 1).astype(jnp.bfloat16)
        parts.append(jnp.concatenate([data_ref[:, :, c * samples:(c + 1) * samples].reshape(rows, samples), mine], axis=1))
        selects.append((row == target + group * c).astype(jnp.bfloat16))
    gathered = jnp.dot(jnp.concatenate(selects, axis=1), jnp.concatenate(parts, axis=0), preferred_element_type=jnp.float32)
    gathered = gathered.astype(jnp.bfloat16)
    acc = jnp.zeros((out_rows, LANES), jnp.float32)
    for first in range(0, taps, 2):
        pair = list(range(first, min(first + 2, taps)))
        tables = jnp.concatenate([table_ref[0, a] for a in pair], axis=1)
        both = jnp.dot(gathered, tables, preferred_element_type=jnp.float32)
        for k, a in enumerate(pair):
            part = both[:, k * samples:(k + 1) * samples]
            shift = stride * (a - reach)
            if shift > 0:
                part = jnp.concatenate([part[shift:], jnp.zeros((shift, LANES), jnp.float32)], axis=0)
            elif shift < 0:
                part = jnp.concatenate([jnp.zeros((-shift, LANES), jnp.float32), part[:shift]], axis=0)
            acc = acc + part
    out_ref[...] = acc.astype(out_ref.dtype)


def fan_call(place, edge, live, block, prev, nxt, tables):
    comps, rows, samples = block.shape
    taps = tables.shape[1]
    kernel = functools.partial(fan_kernel, taps=taps, comps=comps)
    part = pl.BlockSpec((1, rows, samples), lambda c: (c, 0, 0))
    return pl.pallas_call(
        kernel,
        grid=(comps,),
        in_specs=[
            pl.BlockSpec((1, rows), lambda c: (0, 0)),
            pl.BlockSpec((1, LANES), lambda c: (0, 0)),
            pl.BlockSpec((1, rows), lambda c: (0, 0)),
            part,
            part,
            part,
            pl.BlockSpec((1, taps, EXT, LANES), lambda c: (c, 0, 0, 0)),
        ],
        out_specs=pl.BlockSpec((rows // 2, 2, (comps + 1) * LANES), lambda c: (0, 0, 0)),
        out_shape=jax.ShapeDtypeStruct((rows // 2, 2, (comps + 1) * LANES), jnp.bfloat16),
        scratch_shapes=[pltpu.VMEM((rows + 16, EXT), jnp.float32), pltpu.VMEM((rows, LANES), jnp.float32)],
    )(place, edge, live, block, prev, nxt, tables)


def dip_call(target, data, tables, group, comps):
    rows = data.shape[0] * data.shape[1]
    taps = tables.shape[1]
    kernel = functools.partial(dip_kernel, taps=taps, group=group, comps=comps)
    return pl.pallas_call(
        kernel,
        out_shape=jax.ShapeDtypeStruct((rows * comps, LANES), jnp.bfloat16),
    )(target, data, tables)


def on_device(records, fan_taps, dip_taps, live_mask, node_place, shot_place):
    _, comps, nodes, samples = records.shape
    taps = fan_taps.shape[1]
    reach = (taps - 1) // 2
    wide = 2 * reach
    devices = lax.axis_size("shot")
    group = nodes // devices

    block = records[0]
    count = lax.axis_size("tm")
    forward = [(i, i + 1) for i in range(count - 1)]
    backward = [(target, source) for source, target in forward]
    prev = lax.ppermute(block, "tm", forward)
    nxt = lax.ppermute(block, "tm", backward)
    place = lax.axis_index("tm")
    lane = jnp.arange(LANES, dtype=jnp.int32) % wide
    edge = jnp.where(lane < reach, place > 0, place < count - 1).astype(jnp.float32)[None, :]
    packed = fan_call(node_place[None, :], edge, live_mask, block, prev, nxt, circulant(fan_taps, samples))

    data = lax.all_to_all(packed, "shot", split_axis=0, concat_axis=0, tiled=True)
    spread = comps * group
    target = (jnp.repeat(shot_place, group) * spread + jnp.tile(jnp.arange(group, dtype=jnp.int32), devices))[None, :]
    out = dip_call(target, data, circulant(dip_taps[None], samples), group, comps)
    return out.reshape(devices, comps, group, samples)


def solution(mesh):
    return jax.shard_map(
        on_device,
        mesh=mesh,
        in_specs=(P("shot", None, None, "tm"), P(), P(), P("shot", None), P(), P()),
        out_specs=P(None, None, "shot", "tm"),
        check_vma=False,
    )
```

```python
import functools

import jax
import jax.numpy as jnp
from jax import lax
from jax.experimental import pallas as pl
from jax.experimental.pallas import tpu as pltpu
from jax.sharding import PartitionSpec as P

LANES = 128
EXT = 256


def time_halo(block, axis, width):
    count = lax.axis_size(axis)
    forward = [(i, i + 1) for i in range(count - 1)]
    backward = [(target, source) for source, target in forward]
    samples = block.shape[-1]
    low = lax.ppermute(lax.slice_in_dim(block, samples - width, None, axis=-1), axis, forward)
    high = lax.ppermute(lax.slice_in_dim(block, 0, width, axis=-1), axis, backward)
    return low, high


def circulant(tap_set, samples):
    taps = tap_set.shape[-1]
    reach = (taps - 1) // 2
    j = jnp.arange(EXT, dtype=jnp.int32)
    t = jnp.arange(samples, dtype=jnp.int32)
    b = (j[:, None] - t[None, :] + reach) % EXT
    onehot = (b[:, :, None] == jnp.arange(taps, dtype=jnp.int32)[None, None, :]).astype(jnp.bfloat16)
    tables = jnp.einsum("gab,jtb->gajt", tap_set, onehot, preferred_element_type=jnp.float32)
    return tables.astype(jnp.bfloat16)


def fan_kernel(place_ref, edge_ref, ext_ref, table_ref, out_ref, scr_ref, halo_ref, *, taps, live_col, comps):
    c = pl.program_id(0)
    rows = ext_ref.shape[1]
    samples = LANES
    reach = (taps - 1) // 2
    place = place_ref[...]
    select = (lax.broadcasted_iota(jnp.int32, (rows, rows), 0) == place).astype(jnp.bfloat16)
    ordered = jnp.dot(select, ext_ref[0], preferred_element_type=jnp.float32)
    keep = ordered[:, live_col:live_col + 1]
    zeros = jnp.zeros((8, EXT), jnp.float32)
    scr_ref[0:8, :] = zeros
    scr_ref[rows + 8:rows + 16, :] = zeros
    scr_ref[8:rows + 8, :] = ordered
    acc = jnp.zeros((rows, LANES), jnp.float32)
    acc_h = jnp.zeros((rows, LANES), jnp.float32)
    for a in range(taps):
        table = table_ref[0, a]
        both = jnp.concatenate([table, jnp.concatenate([table[samples:], table[:samples]], axis=0)], axis=1)
        moved = scr_ref[pl.ds(a + 8 - reach, rows), :].astype(jnp.bfloat16)
        part = jnp.dot(moved, both, preferred_element_type=jnp.float32)
        acc = acc + part[:, :samples]
        acc_h = acc_h + part[:, samples:]
    out_ref[:, :, pl.ds(pl.multiple_of(c * samples, samples), samples)] = (acc * keep).astype(out_ref.dtype).reshape(rows // 2, 2, samples)
    lane = lax.broadcasted_iota(jnp.int32, (rows, LANES), 1)
    for k in range(comps):
        @pl.when(c == k)
        def _():
            moved = pltpu.roll(acc_h, reach + 2 * reach * k, 1)
            mine = jnp.where((lane >= 2 * reach * k) & (lane < 2 * reach * (k + 1)), moved, 0.0)
            if k == 0:
                halo_ref[...] = mine
            else:
                halo_ref[...] += mine

    @pl.when(c == comps - 1)
    def _():
        out_ref[:, :, comps * samples:(comps + 1) * samples] = (halo_ref[...] * keep * edge_ref[...]).astype(out_ref.dtype).reshape(rows // 2, 2, samples)


def dip_kernel(target_ref, main_ref, halo_ref, table_ref, out_ref, turned_ref, scr_ref, *, taps, comps):
    c = pl.program_id(0)
    devices, group, samples = main_ref.shape
    rows = devices * group
    reach = (taps - 1) // 2
    pad = 16
    target = target_ref[...]
    select = (lax.broadcasted_iota(jnp.int32, (rows, rows), 0) == target).astype(jnp.bfloat16)
    halo = halo_ref[...].reshape(rows, samples).astype(jnp.float32)
    for k in range(comps):
        @pl.when(c == k)
        def _():
            turned_ref[...] = pltpu.roll(halo, (samples - reach - 2 * reach * k) % samples, 1).astype(jnp.bfloat16)

    ext = jnp.concatenate([main_ref[...].reshape(rows, samples), turned_ref[...]], axis=1)
    gathered = jnp.dot(select, ext, preferred_element_type=jnp.float32).astype(jnp.bfloat16)
    zeros = jnp.zeros((pad, EXT), jnp.float32)
    scr_ref[0:pad, :] = zeros
    scr_ref[rows + pad:rows + 2 * pad, :] = zeros
    acc = jnp.zeros((rows, LANES), jnp.float32)
    for first in range(0, taps, 2):
        pair = list(range(first, min(first + 2, taps)))
        tables = jnp.concatenate([table_ref[0, a] for a in pair], axis=1)
        scr_ref[pad:rows + pad, 0:len(pair) * samples] = jnp.dot(gathered, tables, preferred_element_type=jnp.float32)
        for k, a in enumerate(pair):
            acc = acc + scr_ref[pl.ds(pad + group * (a - reach), rows), k * samples:(k + 1) * samples]
    out_ref[:, 0, :, :] = acc.astype(out_ref.dtype).reshape(devices, group, samples)


def fan_call(place, edge, ext, tables, live_col):
    comps, rows, _ = ext.shape
    taps = tables.shape[1]
    kernel = functools.partial(fan_kernel, taps=taps, live_col=live_col, comps=comps)
    return pl.pallas_call(
        kernel,
        grid=(comps,),
        in_specs=[
            pl.BlockSpec((1, rows), lambda c: (0, 0)),
            pl.BlockSpec((1, LANES), lambda c: (0, 0)),
            pl.BlockSpec((1, rows, EXT), lambda c: (c, 0, 0)),
            pl.BlockSpec((1, taps, EXT, LANES), lambda c: (c, 0, 0, 0)),
        ],
        out_specs=pl.BlockSpec((rows // 2, 2, (comps + 1) * LANES), lambda c: (0, 0, 0)),
        out_shape=jax.ShapeDtypeStruct((rows // 2, 2, (comps + 1) * LANES), jnp.bfloat16),
        scratch_shapes=[pltpu.VMEM((rows + 16, EXT), jnp.float32), pltpu.VMEM((rows, LANES), jnp.float32)],
    )(place, edge, ext, tables)


def dip_call(target, data, tables, comps):
    devices, group, _ = data.shape
    taps = tables.shape[1]
    rows = devices * group
    kernel = functools.partial(dip_kernel, taps=taps, comps=comps)
    return pl.pallas_call(
        kernel,
        grid=(comps,),
        in_specs=[
            pl.BlockSpec((1, rows), lambda c: (0, 0)),
            pl.BlockSpec((devices, group, LANES), lambda c: (0, 0, c)),
            pl.BlockSpec((devices, group, LANES), lambda c: (0, 0, comps)),
            pl.BlockSpec((1, taps, EXT, LANES), lambda c: (0, 0, 0, 0)),
        ],
        out_specs=pl.BlockSpec((devices, 1, group, LANES), lambda c: (0, c, 0, 0)),
        out_shape=jax.ShapeDtypeStruct((devices, comps, group, LANES), jnp.bfloat16),
        scratch_shapes=[pltpu.VMEM((rows, LANES), jnp.bfloat16), pltpu.VMEM((rows + 32, EXT), jnp.float32)],
    )(target, data, data, tables)


def on_device(records, fan_taps, dip_taps, live_mask, node_place, shot_place):
    _, comps, nodes, samples = records.shape
    taps = fan_taps.shape[1]
    reach = (taps - 1) // 2
    wide = 2 * reach
    devices = lax.axis_size("shot")
    group = nodes // devices

    block = records[0]
    low, high = time_halo(block, "tm", wide)
    live_col = samples + 32
    live = jnp.broadcast_to(live_mask[0].astype(jnp.bfloat16)[None, :, None], (comps, nodes, 1))
    gap1 = jnp.zeros((comps, nodes, live_col - samples - wide), jnp.bfloat16)
    gap2 = jnp.zeros((comps, nodes, EXT - wide - live_col - 1), jnp.bfloat16)
    ext = jnp.concatenate([block, high, gap1, live, gap2, low], axis=-1)
    place = lax.axis_index("tm")
    lane = jnp.arange(LANES, dtype=jnp.int32) % wide
    edge = jnp.where(lane < reach, place > 0, place < lax.axis_size("tm") - 1).astype(jnp.float32)[None, :]
    packed = fan_call(node_place[None, :], edge, ext, circulant(fan_taps, samples), live_col)

    data = lax.all_to_all(packed, "shot", split_axis=0, concat_axis=0, tiled=True)
    target = (jnp.repeat(shot_place, group) * group + jnp.tile(jnp.arange(group, dtype=jnp.int32), devices))[None, :]
    return dip_call(target, data, circulant(dip_taps[None], samples), comps)


def solution(mesh):
    return jax.shard_map(
        on_device,
        mesh=mesh,
        in_specs=(P("shot", None, None, "tm"), P(), P(), P("shot", None), P(), P()),
        out_specs=P(None, None, "shot", "tm"),
        check_vma=False,
    )
```

```python
import functools

import jax
import jax.numpy as jnp
from jax import lax
from jax.experimental import pallas as pl
from jax.experimental.pallas import tpu as pltpu
from jax.sharding import PartitionSpec as P

LANES = 128
EXT = 256


def time_halo(block, axis, width):
    count = lax.axis_size(axis)
    forward = [(i, i + 1) for i in range(count - 1)]
    backward = [(target, source) for source, target in forward]
    samples = block.shape[-1]
    low = lax.ppermute(lax.slice_in_dim(block, samples - width, None, axis=-1), axis, forward)
    high = lax.ppermute(lax.slice_in_dim(block, 0, width, axis=-1), axis, backward)
    return low, high


def circulant(tap_set, samples):
    taps = tap_set.shape[-1]
    reach = (taps - 1) // 2
    j = jnp.arange(EXT, dtype=jnp.int32)
    t = jnp.arange(samples, dtype=jnp.int32)
    b = (j[:, None] - t[None, :] + reach) % EXT
    onehot = (b[:, :, None] == jnp.arange(taps, dtype=jnp.int32)[None, None, :]).astype(jnp.bfloat16)
    tables = jnp.einsum("gab,jtb->gajt", tap_set, onehot, preferred_element_type=jnp.float32)
    return tables.astype(jnp.bfloat16)


def fan_tables(tap_set, samples):
    taps = tap_set.shape[-1]
    reach = (taps - 1) // 2
    j = jnp.arange(EXT, dtype=jnp.int32)
    t = jnp.arange(samples, dtype=jnp.int32)
    b = (j[:, None] - t[None, :] + reach) % EXT
    onehot = (b[:, :, None] == jnp.arange(taps, dtype=jnp.int32)[None, None, :]).astype(jnp.bfloat16)
    return jnp.einsum("gab,jtb->jgat", tap_set, onehot, preferred_element_type=jnp.float32)


def fan_kernel(place_ref, edge_ref, ext_ref, table_ref, out_ref, scr_ref, halo_ref, *, taps, live_col, comps):
    c = pl.program_id(0)
    rows = ext_ref.shape[1]
    samples = LANES
    reach = (taps - 1) // 2
    place = place_ref[...]
    select = (lax.broadcasted_iota(jnp.int32, (rows, rows), 0) == place).astype(jnp.bfloat16)
    ordered = jnp.dot(select, ext_ref[0], preferred_element_type=jnp.float32)
    keep = ordered[:, live_col:live_col + 1]
    zeros = jnp.zeros((8, EXT), jnp.float32)
    scr_ref[0:8, :] = zeros
    scr_ref[rows + 8:rows + 16, :] = zeros
    scr_ref[8:rows + 8, :] = ordered
    acc = jnp.zeros((rows, LANES), jnp.float32)
    acc_h = jnp.zeros((rows, LANES), jnp.float32)
    for a in range(taps):
        table = table_ref[:, 0, a, :].astype(jnp.bfloat16)
        both = jnp.concatenate([table, jnp.concatenate([table[samples:], table[:samples]], axis=0)], axis=1)
        moved = scr_ref[pl.ds(a + 8 - reach, rows), :].astype(jnp.bfloat16)
        part = jnp.dot(moved, both, preferred_element_type=jnp.float32)
        acc = acc + part[:, :samples]
        acc_h = acc_h + part[:, samples:]
    out_ref[:, :, pl.ds(pl.multiple_of(c * samples, samples), samples)] = (acc * keep).astype(out_ref.dtype).reshape(rows // 2, 2, samples)
    lane = lax.broadcasted_iota(jnp.int32, (rows, LANES), 1)
    for k in range(comps):
        @pl.when(c == k)
        def _():
            moved = pltpu.roll(acc_h, reach + 2 * reach * k, 1)
            mine = jnp.where((lane >= 2 * reach * k) & (lane < 2 * reach * (k + 1)), moved, 0.0)
            if k == 0:
                halo_ref[...] = mine
            else:
                halo_ref[...] += mine

    @pl.when(c == comps - 1)
    def _():
        out_ref[:, :, comps * samples:(comps + 1) * samples] = (halo_ref[...] * keep * edge_ref[...]).astype(out_ref.dtype).reshape(rows // 2, 2, samples)


def dip_kernel(target_ref, data_ref, table_ref, out_ref, *, taps, group, comps):
    rows = data_ref.shape[0] * data_ref.shape[1]
    samples = LANES
    reach = (taps - 1) // 2
    stride = comps * group
    out_rows = out_ref.shape[0]
    target = target_ref[...]
    row = lax.broadcasted_iota(jnp.int32, (out_rows, rows), 0)
    halo = data_ref[:, :, comps * samples:(comps + 1) * samples].reshape(rows, samples).astype(jnp.float32)
    selects, parts = [], []
    for c in range(comps):
        mine = pltpu.roll(halo, (samples - reach - 2 * reach * c) % samples, 1).astype(jnp.bfloat16)
        parts.append(jnp.concatenate([data_ref[:, :, c * samples:(c + 1) * samples].reshape(rows, samples), mine], axis=1))
        selects.append((row == target + group * c).astype(jnp.bfloat16))
    gathered = jnp.dot(jnp.concatenate(selects, axis=1), jnp.concatenate(parts, axis=0), preferred_element_type=jnp.float32)
    gathered = gathered.astype(jnp.bfloat16)
    acc = jnp.zeros((out_rows, LANES), jnp.float32)
    for first in range(0, taps, 2):
        pair = list(range(first, min(first + 2, taps)))
        tables = jnp.concatenate([table_ref[0, a] for a in pair], axis=1)
        both = jnp.dot(gathered, tables, preferred_element_type=jnp.float32)
        for k, a in enumerate(pair):
            part = both[:, k * samples:(k + 1) * samples]
            shift = stride * (a - reach)
            if shift > 0:
                part = jnp.concatenate([part[shift:], jnp.zeros((shift, LANES), jnp.float32)], axis=0)
            elif shift < 0:
                part = jnp.concatenate([jnp.zeros((-shift, LANES), jnp.float32), part[:shift]], axis=0)
            acc = acc + part
    out_ref[...] = acc.astype(out_ref.dtype)


def fan_call(place, edge, ext, tables, live_col):
    comps, rows, _ = ext.shape
    taps = tables.shape[2]
    kernel = functools.partial(fan_kernel, taps=taps, live_col=live_col, comps=comps)
    return pl.pallas_call(
        kernel,
        grid=(comps,),
        in_specs=[
            pl.BlockSpec((1, rows), lambda c: (0, 0)),
            pl.BlockSpec((1, LANES), lambda c: (0, 0)),
            pl.BlockSpec((1, rows, EXT), lambda c: (c, 0, 0)),
            pl.BlockSpec((EXT, 1, taps, LANES), lambda c: (0, c, 0, 0)),
        ],
        out_specs=pl.BlockSpec((rows // 2, 2, (comps + 1) * LANES), lambda c: (0, 0, 0)),
        out_shape=jax.ShapeDtypeStruct((rows // 2, 2, (comps + 1) * LANES), jnp.bfloat16),
        scratch_shapes=[pltpu.VMEM((rows + 16, EXT), jnp.float32), pltpu.VMEM((rows, LANES), jnp.float32)],
    )(place, edge, ext, tables)


def dip_call(target, data, tables, group, comps):
    rows = data.shape[0] * data.shape[1]
    taps = tables.shape[1]
    kernel = functools.partial(dip_kernel, taps=taps, group=group, comps=comps)
    return pl.pallas_call(
        kernel,
        out_shape=jax.ShapeDtypeStruct((rows * comps, LANES), jnp.bfloat16),
    )(target, data, tables)


def on_device(records, fan_taps, dip_taps, live_mask, node_place, shot_place):
    _, comps, nodes, samples = records.shape
    taps = fan_taps.shape[1]
    reach = (taps - 1) // 2
    wide = 2 * reach
    devices = lax.axis_size("shot")
    group = nodes // devices

    block = records[0]
    low, high = time_halo(block, "tm", wide)
    live_col = samples + 32
    live = jnp.broadcast_to(live_mask[0].astype(jnp.bfloat16)[None, :, None], (comps, nodes, 1))
    gap1 = jnp.zeros((comps, nodes, live_col - samples - wide), jnp.bfloat16)
    gap2 = jnp.zeros((comps, nodes, EXT - wide - live_col - 1), jnp.bfloat16)
    ext = jnp.concatenate([block, high, gap1, live, gap2, low], axis=-1)
    place = lax.axis_index("tm")
    lane = jnp.arange(LANES, dtype=jnp.int32) % wide
    edge = jnp.where(lane < reach, place > 0, place < lax.axis_size("tm") - 1).astype(jnp.float32)[None, :]
    packed = fan_call(node_place[None, :], edge, ext, fan_tables(fan_taps, samples), live_col)

    data = lax.all_to_all(packed, "shot", split_axis=0, concat_axis=0, tiled=True)
    spread = comps * group
    target = (jnp.repeat(shot_place, group) * spread + jnp.tile(jnp.arange(group, dtype=jnp.int32), devices))[None, :]
    out = dip_call(target, data, circulant(dip_taps[None], samples), group, comps)
    return out.reshape(devices, comps, group, samples)


def solution(mesh):
    return jax.shard_map(
        on_device,
        mesh=mesh,
        in_specs=(P("shot", None, None, "tm"), P(), P(), P("shot", None), P(), P()),
        out_specs=P(None, None, "shot", "tm"),
        check_vma=False,
    )
```

```python
import functools

import jax
import jax.numpy as jnp
from jax import lax
from jax.experimental import pallas as pl
from jax.experimental.pallas import tpu as pltpu
from jax.sharding import PartitionSpec as P

LANES = 128
EXT = 256


def time_halo(block, axis, width):
    count = lax.axis_size(axis)
    forward = [(i, i + 1) for i in range(count - 1)]
    backward = [(target, source) for source, target in forward]
    samples = block.shape[-1]
    low = lax.ppermute(lax.slice_in_dim(block, samples - width, None, axis=-1), axis, forward)
    high = lax.ppermute(lax.slice_in_dim(block, 0, width, axis=-1), axis, backward)
    return low, high


def circulant(tap_set, samples):
    taps = tap_set.shape[-1]
    reach = (taps - 1) // 2
    j = jnp.arange(EXT, dtype=jnp.int32)
    t = jnp.arange(samples, dtype=jnp.int32)
    b = (j[:, None] - t[None, :] + reach) % EXT
    onehot = (b[:, :, None] == jnp.arange(taps, dtype=jnp.int32)[None, None, :]).astype(jnp.bfloat16)
    tables = jnp.einsum("gab,jtb->gajt", tap_set, onehot, preferred_element_type=jnp.float32)
    return tables.astype(jnp.bfloat16)


def fan_kernel(place_ref, edge_ref, ext_ref, table_ref, out_ref, scr_ref, halo_ref, *, taps, live_col, comps):
    c = pl.program_id(0)
    rows = ext_ref.shape[1]
    samples = LANES
    reach = (taps - 1) // 2
    place = place_ref[...]
    select = (lax.broadcasted_iota(jnp.int32, (rows, rows), 0) == place).astype(jnp.bfloat16)
    ordered = jnp.dot(select, ext_ref[0], preferred_element_type=jnp.float32)
    keep = ordered[:, live_col:live_col + 1]
    zeros = jnp.zeros((8, EXT), jnp.float32)
    scr_ref[0:8, :] = zeros
    scr_ref[rows + 8:rows + 16, :] = zeros
    scr_ref[8:rows + 8, :] = ordered
    acc = jnp.zeros((rows, LANES), jnp.float32)
    acc_h = jnp.zeros((rows, LANES), jnp.float32)
    for a in range(taps):
        table = table_ref[0, a]
        both = jnp.concatenate([table, jnp.concatenate([table[samples:], table[:samples]], axis=0)], axis=1)
        moved = scr_ref[pl.ds(a + 8 - reach, rows), :].astype(jnp.bfloat16)
        part = jnp.dot(moved, both, preferred_element_type=jnp.float32)
        acc = acc + part[:, :samples]
        acc_h = acc_h + part[:, samples:]
    out_ref[:, :, pl.ds(pl.multiple_of(c * samples, samples), samples)] = (acc * keep).astype(out_ref.dtype).reshape(rows // 2, 2, samples)
    lane = lax.broadcasted_iota(jnp.int32, (rows, LANES), 1)
    for k in range(comps):
        @pl.when(c == k)
        def _():
            moved = pltpu.roll(acc_h, reach + 2 * reach * k, 1)
            mine = jnp.where((lane >= 2 * reach * k) & (lane < 2 * reach * (k + 1)), moved, 0.0)
            if k == 0:
                halo_ref[...] = mine
            else:
                halo_ref[...] += mine

    @pl.when(c == comps - 1)
    def _():
        out_ref[:, :, comps * samples:(comps + 1) * samples] = (halo_ref[...] * keep * edge_ref[...]).astype(out_ref.dtype).reshape(rows // 2, 2, samples)


def dip_kernel(select_ref, data_ref, table_ref, out_ref, *, taps, group, comps):
    rows = data_ref.shape[0] * data_ref.shape[1]
    samples = LANES
    reach = (taps - 1) // 2
    stride = comps * group
    out_rows = out_ref.shape[0]
    halo = data_ref[:, :, comps * samples:(comps + 1) * samples].reshape(rows, samples).astype(jnp.float32)
    parts = []
    for c in range(comps):
        mine = pltpu.roll(halo, (samples - reach - 2 * reach * c) % samples, 1).astype(jnp.bfloat16)
        parts.append(jnp.concatenate([data_ref[:, :, c * samples:(c + 1) * samples].reshape(rows, samples), mine], axis=1))
    gathered = jnp.dot(select_ref[...], jnp.concatenate(parts, axis=0), preferred_element_type=jnp.float32)
    gathered = gathered.astype(jnp.bfloat16)
    acc = jnp.zeros((out_rows, LANES), jnp.float32)
    for first in range(0, taps, 2):
        pair = list(range(first, min(first + 2, taps)))
        tables = jnp.concatenate([table_ref[0, a] for a in pair], axis=1)
        both = jnp.dot(gathered, tables, preferred_element_type=jnp.float32)
        for k, a in enumerate(pair):
            part = both[:, k * samples:(k + 1) * samples]
            shift = stride * (a - reach)
            if shift > 0:
                part = jnp.concatenate([part[shift:], jnp.zeros((shift, LANES), jnp.float32)], axis=0)
            elif shift < 0:
                part = jnp.concatenate([jnp.zeros((-shift, LANES), jnp.float32), part[:shift]], axis=0)
            acc = acc + part
    out_ref[...] = acc.astype(out_ref.dtype)


def fan_call(place, edge, ext, tables, live_col):
    comps, rows, _ = ext.shape
    taps = tables.shape[1]
    kernel = functools.partial(fan_kernel, taps=taps, live_col=live_col, comps=comps)
    return pl.pallas_call(
        kernel,
        grid=(comps,),
        in_specs=[
            pl.BlockSpec((1, rows), lambda c: (0, 0)),
            pl.BlockSpec((1, LANES), lambda c: (0, 0)),
            pl.BlockSpec((1, rows, EXT), lambda c: (c, 0, 0)),
            pl.BlockSpec((1, taps, EXT, LANES), lambda c: (c, 0, 0, 0)),
        ],
        out_specs=pl.BlockSpec((rows // 2, 2, (comps + 1) * LANES), lambda c: (0, 0, 0)),
        out_shape=jax.ShapeDtypeStruct((rows // 2, 2, (comps + 1) * LANES), jnp.bfloat16),
        scratch_shapes=[pltpu.VMEM((rows + 16, EXT), jnp.float32), pltpu.VMEM((rows, LANES), jnp.float32)],
    )(place, edge, ext, tables)


def dip_call(select, data, tables, group, comps):
    rows = data.shape[0] * data.shape[1]
    taps = tables.shape[1]
    kernel = functools.partial(dip_kernel, taps=taps, group=group, comps=comps)
    return pl.pallas_call(
        kernel,
        out_shape=jax.ShapeDtypeStruct((rows * comps, LANES), jnp.bfloat16),
    )(select, data, tables)


def on_device(records, fan_taps, dip_taps, live_mask, node_place, shot_place):
    _, comps, nodes, samples = records.shape
    taps = fan_taps.shape[1]
    reach = (taps - 1) // 2
    wide = 2 * reach
    devices = lax.axis_size("shot")
    group = nodes // devices

    block = records[0]
    low, high = time_halo(block, "tm", wide)
    live_col = samples + 32
    live = jnp.broadcast_to(live_mask[0].astype(jnp.bfloat16)[None, :, None], (comps, nodes, 1))
    gap1 = jnp.zeros((comps, nodes, live_col - samples - wide), jnp.bfloat16)
    gap2 = jnp.zeros((comps, nodes, EXT - wide - live_col - 1), jnp.bfloat16)
    ext = jnp.concatenate([block, high, gap1, live, gap2, low], axis=-1)
    place = lax.axis_index("tm")
    lane = jnp.arange(LANES, dtype=jnp.int32) % wide
    edge = jnp.where(lane < reach, place > 0, place < lax.axis_size("tm") - 1).astype(jnp.float32)[None, :]
    packed = fan_call(node_place[None, :], edge, ext, circulant(fan_taps, samples), live_col)

    data = lax.all_to_all(packed, "shot", split_axis=0, concat_axis=0, tiled=True)
    spread = comps * group
    target = (jnp.repeat(shot_place, group) * spread + jnp.tile(jnp.arange(group, dtype=jnp.int32), devices))[None, :]
    row = jnp.arange(devices * spread, dtype=jnp.int32)[:, None]
    select = jnp.concatenate([(row == target + group * c).astype(jnp.bfloat16) for c in range(comps)], axis=1)
    out = dip_call(select, data, circulant(dip_taps[None], samples), group, comps)
    return out.reshape(devices, comps, group, samples)


def solution(mesh):
    return jax.shard_map(
        on_device,
        mesh=mesh,
        in_specs=(P("shot", None, None, "tm"), P(), P(), P("shot", None), P(), P()),
        out_specs=P(None, None, "shot", "tm"),
        check_vma=False,
    )
```

```python
import functools

import jax
import jax.numpy as jnp
from jax import lax
from jax.experimental import pallas as pl
from jax.experimental.pallas import tpu as pltpu
from jax.sharding import PartitionSpec as P

LANES = 128
EXT = 256


def time_halo(block, axis, width):
    count = lax.axis_size(axis)
    forward = [(i, i + 1) for i in range(count - 1)]
    backward = [(target, source) for source, target in forward]
    samples = block.shape[-1]
    low = lax.ppermute(lax.slice_in_dim(block, samples - width, None, axis=-1), axis, forward)
    high = lax.ppermute(lax.slice_in_dim(block, 0, width, axis=-1), axis, backward)
    return low, high


def circulant(tap_set, samples):
    taps = tap_set.shape[-1]
    reach = (taps - 1) // 2
    j = jnp.arange(EXT, dtype=jnp.int32)
    t = jnp.arange(samples, dtype=jnp.int32)
    b = (j[:, None] - t[None, :] + reach) % EXT
    onehot = (b[:, :, None] == jnp.arange(taps, dtype=jnp.int32)[None, None, :]).astype(jnp.bfloat16)
    tables = jnp.einsum("gab,jtb->gajt", tap_set, onehot, preferred_element_type=jnp.float32)
    return tables.astype(jnp.bfloat16)


def fan_kernel(place_ref, edge_ref, ext_ref, table_ref, out_ref, scr_ref, halo_ref, *, taps, live_col, comps):
    c = pl.program_id(0)
    rows = ext_ref.shape[1]
    samples = LANES
    reach = (taps - 1) // 2
    place = place_ref[...]
    select = (lax.broadcasted_iota(jnp.int32, (rows, rows), 0) == place).astype(jnp.bfloat16)
    ordered = jnp.dot(select, ext_ref[0], preferred_element_type=jnp.float32)
    keep = ordered[:, live_col:live_col + 1]
    zeros = jnp.zeros((8, EXT), jnp.float32)
    scr_ref[0:8, :] = zeros
    scr_ref[rows + 8:rows + 16, :] = zeros
    scr_ref[8:rows + 8, :] = ordered
    acc = jnp.zeros((rows, LANES), jnp.float32)
    acc_h = jnp.zeros((rows, LANES), jnp.float32)
    for a in range(taps):
        table = table_ref[0, a]
        both = jnp.concatenate([table, jnp.concatenate([table[samples:], table[:samples]], axis=0)], axis=1)
        moved = scr_ref[pl.ds(a + 8 - reach, rows), :].astype(jnp.bfloat16)
        part = jnp.dot(moved, both, preferred_element_type=jnp.float32)
        acc = acc + part[:, :samples]
        acc_h = acc_h + part[:, samples:]
    out_ref[:, :, pl.ds(pl.multiple_of(c * samples, samples), samples)] = (acc * keep).astype(out_ref.dtype).reshape(rows // 2, 2, samples)
    lane = lax.broadcasted_iota(jnp.int32, (rows, LANES), 1)
    for k in range(comps):
        @pl.when(c == k)
        def _():
            moved = pltpu.roll(acc_h, reach + 2 * reach * k, 1)
            mine = jnp.where((lane >= 2 * reach * k) & (lane < 2 * reach * (k + 1)), moved, 0.0)
            if k == 0:
                halo_ref[...] = mine
            else:
                halo_ref[...] += mine

    @pl.when(c == comps - 1)
    def _():
        out_ref[:, :, comps * samples:(comps + 1) * samples] = (halo_ref[...] * keep * edge_ref[...]).astype(out_ref.dtype).reshape(rows // 2, 2, samples)


def dip_kernel(target_ref, data_ref, table_ref, out_ref, *, taps, group, comps):
    rows = data_ref.shape[0] * data_ref.shape[1]
    samples = LANES
    reach = (taps - 1) // 2
    stride = comps * group
    out_rows = out_ref.shape[0]
    target = target_ref[...]
    row = lax.broadcasted_iota(jnp.int32, (out_rows, rows), 0)
    halo = data_ref[:, :, comps * samples:(comps + 1) * samples].reshape(rows, samples).astype(jnp.float32)
    selects, parts = [], []
    for c in range(comps):
        mine = pltpu.roll(halo, (samples - reach - 2 * reach * c) % samples, 1).astype(jnp.bfloat16)
        parts.append(jnp.concatenate([data_ref[:, :, c * samples:(c + 1) * samples].reshape(rows, samples), mine], axis=1))
        selects.append((row == target + group * c).astype(jnp.bfloat16))
    gathered = sum(jnp.dot(sel, part, preferred_element_type=jnp.float32) for sel, part in zip(selects, parts))
    gathered = gathered.astype(jnp.bfloat16)
    acc = jnp.zeros((out_rows, LANES), jnp.float32)
    for first in range(0, taps, 2):
        pair = list(range(first, min(first + 2, taps)))
        tables = jnp.concatenate([table_ref[0, a] for a in pair], axis=1)
        both = jnp.dot(gathered, tables, preferred_element_type=jnp.float32)
        for k, a in enumerate(pair):
            part = both[:, k * samples:(k + 1) * samples]
            shift = stride * (a - reach)
            if shift > 0:
                part = jnp.concatenate([part[shift:], jnp.zeros((shift, LANES), jnp.float32)], axis=0)
            elif shift < 0:
                part = jnp.concatenate([jnp.zeros((-shift, LANES), jnp.float32), part[:shift]], axis=0)
            acc = acc + part
    out_ref[...] = acc.astype(out_ref.dtype)


def fan_call(place, edge, ext, tables, live_col):
    comps, rows, _ = ext.shape
    taps = tables.shape[1]
    kernel = functools.partial(fan_kernel, taps=taps, live_col=live_col, comps=comps)
    return pl.pallas_call(
        kernel,
        grid=(comps,),
        in_specs=[
            pl.BlockSpec((1, rows), lambda c: (0, 0)),
            pl.BlockSpec((1, LANES), lambda c: (0, 0)),
            pl.BlockSpec((1, rows, EXT), lambda c: (c, 0, 0)),
            pl.BlockSpec((1, taps, EXT, LANES), lambda c: (c, 0, 0, 0)),
        ],
        out_specs=pl.BlockSpec((rows // 2, 2, (comps + 1) * LANES), lambda c: (0, 0, 0)),
        out_shape=jax.ShapeDtypeStruct((rows // 2, 2, (comps + 1) * LANES), jnp.bfloat16),
        scratch_shapes=[pltpu.VMEM((rows + 16, EXT), jnp.float32), pltpu.VMEM((rows, LANES), jnp.float32)],
    )(place, edge, ext, tables)


def dip_call(target, data, tables, group, comps):
    rows = data.shape[0] * data.shape[1]
    taps = tables.shape[1]
    kernel = functools.partial(dip_kernel, taps=taps, group=group, comps=comps)
    return pl.pallas_call(
        kernel,
        out_shape=jax.ShapeDtypeStruct((rows * comps, LANES), jnp.bfloat16),
    )(target, data, tables)


def on_device(records, fan_taps, dip_taps, live_mask, node_place, shot_place):
    _, comps, nodes, samples = records.shape
    taps = fan_taps.shape[1]
    reach = (taps - 1) // 2
    wide = 2 * reach
    devices = lax.axis_size("shot")
    group = nodes // devices

    block = records[0]
    low, high = time_halo(block, "tm", wide)
    live_col = samples + 32
    live = jnp.broadcast_to(live_mask[0].astype(jnp.bfloat16)[None, :, None], (comps, nodes, 1))
    gap1 = jnp.zeros((comps, nodes, live_col - samples - wide), jnp.bfloat16)
    gap2 = jnp.zeros((comps, nodes, EXT - wide - live_col - 1), jnp.bfloat16)
    ext = jnp.concatenate([block, high, gap1, live, gap2, low], axis=-1)
    place = lax.axis_index("tm")
    lane = jnp.arange(LANES, dtype=jnp.int32) % wide
    edge = jnp.where(lane < reach, place > 0, place < lax.axis_size("tm") - 1).astype(jnp.float32)[None, :]
    packed = fan_call(node_place[None, :], edge, ext, circulant(fan_taps, samples), live_col)

    data = lax.all_to_all(packed, "shot", split_axis=0, concat_axis=0, tiled=True)
    spread = comps * group
    target = (jnp.repeat(shot_place, group) * spread + jnp.tile(jnp.arange(group, dtype=jnp.int32), devices))[None, :]
    out = dip_call(target, data, circulant(dip_taps[None], samples), group, comps)
    return out.reshape(devices, comps, group, samples)


def solution(mesh):
    return jax.shard_map(
        on_device,
        mesh=mesh,
        in_specs=(P("shot", None, None, "tm"), P(), P(), P("shot", None), P(), P()),
        out_specs=P(None, None, "shot", "tm"),
        check_vma=False,
    )
```

```python
import functools

import jax
import jax.numpy as jnp
from jax import lax
from jax.experimental import pallas as pl
from jax.experimental.pallas import tpu as pltpu
from jax.sharding import PartitionSpec as P

LANES = 128
EXT = 256


def time_halo(block, axis, width):
    count = lax.axis_size(axis)
    forward = [(i, i + 1) for i in range(count - 1)]
    backward = [(target, source) for source, target in forward]
    samples = block.shape[-1]
    low = lax.ppermute(lax.slice_in_dim(block, samples - width, None, axis=-1), axis, forward)
    high = lax.ppermute(lax.slice_in_dim(block, 0, width, axis=-1), axis, backward)
    return low, high


def circulant(tap_set, samples):
    taps = tap_set.shape[-1]
    reach = (taps - 1) // 2
    j = jnp.arange(EXT, dtype=jnp.int32)
    t = jnp.arange(samples, dtype=jnp.int32)
    b = (j[:, None] - t[None, :] + reach) % EXT
    onehot = (b[:, :, None] == jnp.arange(taps, dtype=jnp.int32)[None, None, :]).astype(jnp.bfloat16)
    tables = jnp.einsum("gab,jtb->gajt", tap_set, onehot, preferred_element_type=jnp.float32)
    return tables.astype(jnp.bfloat16)


def fan_kernel(place_ref, edge_ref, ext_ref, table_ref, out_ref, scr_ref, halo_ref, *, taps, live_col, comps):
    c = pl.program_id(0)
    rows = ext_ref.shape[1]
    samples = LANES
    reach = (taps - 1) // 2
    place = place_ref[...]
    select = (lax.broadcasted_iota(jnp.int32, (rows, rows), 0) == place).astype(jnp.bfloat16)
    ordered = jnp.dot(select, ext_ref[0], preferred_element_type=jnp.float32)
    keep = ordered[:, live_col:live_col + 1]
    zeros = jnp.zeros((8, EXT), jnp.float32)
    scr_ref[0:8, :] = zeros
    scr_ref[rows + 8:rows + 16, :] = zeros
    scr_ref[8:rows + 8, :] = ordered
    acc = jnp.zeros((rows, LANES), jnp.float32)
    acc_h = jnp.zeros((rows, LANES), jnp.float32)
    for a in range(taps):
        table = table_ref[0, a]
        both = jnp.concatenate([table, jnp.concatenate([table[samples:], table[:samples]], axis=0)], axis=1)
        moved = scr_ref[pl.ds(a + 8 - reach, rows), :].astype(jnp.bfloat16)
        part = jnp.dot(moved, both, preferred_element_type=jnp.float32)
        acc = acc + part[:, :samples]
        acc_h = acc_h + part[:, samples:]
    out_ref[:, :, pl.ds(pl.multiple_of(c * samples, samples), samples)] = (acc * keep).astype(out_ref.dtype).reshape(rows // 2, 2, samples)
    lane = lax.broadcasted_iota(jnp.int32, (rows, LANES), 1)
    for k in range(comps):
        @pl.when(c == k)
        def _():
            moved = pltpu.roll(acc_h, reach + 2 * reach * k, 1)
            mine = jnp.where((lane >= 2 * reach * k) & (lane < 2 * reach * (k + 1)), moved, 0.0)
            if k == 0:
                halo_ref[...] = mine
            else:
                halo_ref[...] += mine

    @pl.when(c == comps - 1)
    def _():
        out_ref[:, :, comps * samples:(comps + 1) * samples] = (halo_ref[...] * keep * edge_ref[...]).astype(out_ref.dtype).reshape(rows // 2, 2, samples)


def dip_kernel(target_ref, source_ref, table_ref, out_ref, data_ref, sem, *, taps, group, comps):
    fetch = pltpu.make_async_copy(source_ref, data_ref, sem)
    fetch.start()
    rows = data_ref.shape[0] * data_ref.shape[1]
    samples = LANES
    reach = (taps - 1) // 2
    stride = comps * group
    out_rows = out_ref.shape[0]
    target = target_ref[...]
    row = lax.broadcasted_iota(jnp.int32, (out_rows, rows), 0)
    selects = [(row == target + group * c).astype(jnp.bfloat16) for c in range(comps)]
    fetch.wait()
    halo = data_ref[:, :, comps * samples:(comps + 1) * samples].reshape(rows, samples).astype(jnp.float32)
    parts = []
    for c in range(comps):
        mine = pltpu.roll(halo, (samples - reach - 2 * reach * c) % samples, 1).astype(jnp.bfloat16)
        parts.append(jnp.concatenate([data_ref[:, :, c * samples:(c + 1) * samples].reshape(rows, samples), mine], axis=1))
    gathered = jnp.dot(jnp.concatenate(selects, axis=1), jnp.concatenate(parts, axis=0), preferred_element_type=jnp.float32)
    gathered = gathered.astype(jnp.bfloat16)
    acc = jnp.zeros((out_rows, LANES), jnp.float32)
    for first in range(0, taps, 2):
        pair = list(range(first, min(first + 2, taps)))
        tables = jnp.concatenate([table_ref[0, a] for a in pair], axis=1)
        both = jnp.dot(gathered, tables, preferred_element_type=jnp.float32)
        for k, a in enumerate(pair):
            part = both[:, k * samples:(k + 1) * samples]
            shift = stride * (a - reach)
            if shift > 0:
                part = jnp.concatenate([part[shift:], jnp.zeros((shift, LANES), jnp.float32)], axis=0)
            elif shift < 0:
                part = jnp.concatenate([jnp.zeros((-shift, LANES), jnp.float32), part[:shift]], axis=0)
            acc = acc + part
    out_ref[...] = acc.astype(out_ref.dtype)


def fan_call(place, edge, ext, tables, live_col):
    comps, rows, _ = ext.shape
    taps = tables.shape[1]
    kernel = functools.partial(fan_kernel, taps=taps, live_col=live_col, comps=comps)
    return pl.pallas_call(
        kernel,
        grid=(comps,),
        in_specs=[
            pl.BlockSpec((1, rows), lambda c: (0, 0)),
            pl.BlockSpec((1, LANES), lambda c: (0, 0)),
            pl.BlockSpec((1, rows, EXT), lambda c: (c, 0, 0)),
            pl.BlockSpec((1, taps, EXT, LANES), lambda c: (c, 0, 0, 0)),
        ],
        out_specs=pl.BlockSpec((rows // 2, 2, (comps + 1) * LANES), lambda c: (0, 0, 0)),
        out_shape=jax.ShapeDtypeStruct((rows // 2, 2, (comps + 1) * LANES), jnp.bfloat16),
        scratch_shapes=[pltpu.VMEM((rows + 16, EXT), jnp.float32), pltpu.VMEM((rows, LANES), jnp.float32)],
    )(place, edge, ext, tables)


def dip_call(target, data, tables, group, comps):
    rows = data.shape[0] * data.shape[1]
    taps = tables.shape[1]
    kernel = functools.partial(dip_kernel, taps=taps, group=group, comps=comps)
    vmem = pl.BlockSpec(memory_space=pltpu.VMEM)
    return pl.pallas_call(
        kernel,
        in_specs=[vmem, pl.BlockSpec(memory_space=pl.ANY), vmem],
        out_specs=vmem,
        out_shape=jax.ShapeDtypeStruct((rows * comps, LANES), jnp.bfloat16),
        scratch_shapes=[pltpu.VMEM(data.shape, data.dtype), pltpu.SemaphoreType.DMA(())],
    )(target, data, tables)


def on_device(records, fan_taps, dip_taps, live_mask, node_place, shot_place):
    _, comps, nodes, samples = records.shape
    taps = fan_taps.shape[1]
    reach = (taps - 1) // 2
    wide = 2 * reach
    devices = lax.axis_size("shot")
    group = nodes // devices

    block = records[0]
    low, high = time_halo(block, "tm", wide)
    live_col = samples + 32
    live = jnp.broadcast_to(live_mask[0].astype(jnp.bfloat16)[None, :, None], (comps, nodes, 1))
    gap1 = jnp.zeros((comps, nodes, live_col - samples - wide), jnp.bfloat16)
    gap2 = jnp.zeros((comps, nodes, EXT - wide - live_col - 1), jnp.bfloat16)
    ext = jnp.concatenate([block, high, gap1, live, gap2, low], axis=-1)
    place = lax.axis_index("tm")
    lane = jnp.arange(LANES, dtype=jnp.int32) % wide
    edge = jnp.where(lane < reach, place > 0, place < lax.axis_size("tm") - 1).astype(jnp.float32)[None, :]
    packed = fan_call(node_place[None, :], edge, ext, circulant(fan_taps, samples), live_col)

    data = lax.all_to_all(packed, "shot", split_axis=0, concat_axis=0, tiled=True)
    spread = comps * group
    target = (jnp.repeat(shot_place, group) * spread + jnp.tile(jnp.arange(group, dtype=jnp.int32), devices))[None, :]
    out = dip_call(target, data, circulant(dip_taps[None], samples), group, comps)
    return out.reshape(devices, comps, group, samples)


def solution(mesh):
    return jax.shard_map(
        on_device,
        mesh=mesh,
        in_specs=(P("shot", None, None, "tm"), P(), P(), P("shot", None), P(), P()),
        out_specs=P(None, None, "shot", "tm"),
        check_vma=False,
    )
```

```python
import functools

import jax
import jax.numpy as jnp
from jax import lax
from jax.experimental import pallas as pl
from jax.experimental.pallas import tpu as pltpu
from jax.sharding import PartitionSpec as P

LANES = 128
EXT = 256


def time_halo(block, axis, width):
    count = lax.axis_size(axis)
    forward = [(i, i + 1) for i in range(count - 1)]
    backward = [(target, source) for source, target in forward]
    samples = block.shape[-1]
    low = lax.ppermute(lax.slice_in_dim(block, samples - width, None, axis=-1), axis, forward)
    high = lax.ppermute(lax.slice_in_dim(block, 0, width, axis=-1), axis, backward)
    return low, high


def circulant(tap_set, samples):
    taps = tap_set.shape[-1]
    reach = (taps - 1) // 2
    j = jnp.arange(EXT, dtype=jnp.int32)
    t = jnp.arange(samples, dtype=jnp.int32)
    b = (j[:, None] - t[None, :] + reach) % EXT
    onehot = (b[:, :, None] == jnp.arange(taps, dtype=jnp.int32)[None, None, :]).astype(jnp.bfloat16)
    tables = jnp.einsum("gab,jtb->gajt", tap_set, onehot, preferred_element_type=jnp.float32)
    return tables.astype(jnp.bfloat16)


def fan_kernel(place_ref, edge_ref, ext_ref, table_ref, out_ref, scr_ref, halo_ref, *, taps, live_col, comps):
    c = pl.program_id(0)
    rows = ext_ref.shape[1]
    samples = LANES
    reach = (taps - 1) // 2
    place = place_ref[...]
    select = (lax.broadcasted_iota(jnp.int32, (rows, rows), 0) == place).astype(jnp.bfloat16)
    ordered = jnp.dot(select, ext_ref[0], preferred_element_type=jnp.float32)
    keep = ordered[:, live_col:live_col + 1]
    zeros = jnp.zeros((8, EXT), jnp.float32)
    scr_ref[0:8, :] = zeros
    scr_ref[rows + 8:rows + 16, :] = zeros
    scr_ref[8:rows + 8, :] = ordered
    acc = jnp.zeros((rows, LANES), jnp.float32)
    acc_h = jnp.zeros((rows, LANES), jnp.float32)
    for a in range(taps):
        table = table_ref[0, a]
        both = jnp.concatenate([table, jnp.concatenate([table[samples:], table[:samples]], axis=0)], axis=1)
        moved = scr_ref[pl.ds(a + 8 - reach, rows), :].astype(jnp.bfloat16)
        part = jnp.dot(moved, both, preferred_element_type=jnp.float32)
        acc = acc + part[:, :samples]
        acc_h = acc_h + part[:, samples:]
    out_ref[:, :, pl.ds(pl.multiple_of(c * samples, samples), samples)] = (acc * keep).astype(out_ref.dtype).reshape(rows // 2, 2, samples)
    lane = lax.broadcasted_iota(jnp.int32, (rows, LANES), 1)
    for k in range(comps):
        @pl.when(c == k)
        def _():
            moved = pltpu.roll(acc_h, reach + 2 * reach * k, 1)
            mine = jnp.where((lane >= 2 * reach * k) & (lane < 2 * reach * (k + 1)), moved, 0.0)
            if k == 0:
                halo_ref[...] = mine
            else:
                halo_ref[...] += mine

    @pl.when(c == comps - 1)
    def _():
        out_ref[:, :, comps * samples:(comps + 1) * samples] = (halo_ref[...] * keep * edge_ref[...]).astype(out_ref.dtype).reshape(rows // 2, 2, samples)


def dip_kernel(target_ref, data_ref, table_ref, out_ref, acc_ref, *, taps, group, comps):
    rows = data_ref.shape[0] * data_ref.shape[1]
    samples = LANES
    reach = (taps - 1) // 2
    stride = comps * group
    out_rows = out_ref.shape[0]
    target = target_ref[...]
    row = lax.broadcasted_iota(jnp.int32, (out_rows, rows), 0)
    halo = data_ref[:, :, comps * samples:(comps + 1) * samples].reshape(rows, samples).astype(jnp.float32)
    selects, parts = [], []
    for c in range(comps):
        mine = pltpu.roll(halo, (samples - reach - 2 * reach * c) % samples, 1).astype(jnp.bfloat16)
        parts.append(jnp.concatenate([data_ref[:, :, c * samples:(c + 1) * samples].reshape(rows, samples), mine], axis=1))
        selects.append((row == target + group * c).astype(jnp.bfloat16))
    gathered = jnp.dot(jnp.concatenate(selects, axis=1), jnp.concatenate(parts, axis=0), preferred_element_type=jnp.float32)
    gathered = gathered.astype(jnp.bfloat16)
    acc_ref[...] = jnp.zeros((out_rows, LANES), jnp.float32)
    for first in range(0, taps, 2):
        pair = list(range(first, min(first + 2, taps)))
        tables = jnp.concatenate([table_ref[0, a] for a in pair], axis=1)
        both = jnp.dot(gathered, tables, preferred_element_type=jnp.float32)
        for k, a in enumerate(pair):
            shift = stride * (a - reach)
            lo, hi = max(0, -shift), out_rows - max(0, shift)
            acc_ref[lo:hi, :] += both[lo + shift:hi + shift, k * samples:(k + 1) * samples]
    out_ref[...] = acc_ref[...].astype(out_ref.dtype)


def fan_call(place, edge, ext, tables, live_col):
    comps, rows, _ = ext.shape
    taps = tables.shape[1]
    kernel = functools.partial(fan_kernel, taps=taps, live_col=live_col, comps=comps)
    return pl.pallas_call(
        kernel,
        grid=(comps,),
        in_specs=[
            pl.BlockSpec((1, rows), lambda c: (0, 0)),
            pl.BlockSpec((1, LANES), lambda c: (0, 0)),
            pl.BlockSpec((1, rows, EXT), lambda c: (c, 0, 0)),
            pl.BlockSpec((1, taps, EXT, LANES), lambda c: (c, 0, 0, 0)),
        ],
        out_specs=pl.BlockSpec((rows // 2, 2, (comps + 1) * LANES), lambda c: (0, 0, 0)),
        out_shape=jax.ShapeDtypeStruct((rows // 2, 2, (comps + 1) * LANES), jnp.bfloat16),
        scratch_shapes=[pltpu.VMEM((rows + 16, EXT), jnp.float32), pltpu.VMEM((rows, LANES), jnp.float32)],
    )(place, edge, ext, tables)


def dip_call(target, data, tables, group, comps):
    rows = data.shape[0] * data.shape[1]
    taps = tables.shape[1]
    kernel = functools.partial(dip_kernel, taps=taps, group=group, comps=comps)
    return pl.pallas_call(
        kernel,
        out_shape=jax.ShapeDtypeStruct((rows * comps, LANES), jnp.bfloat16),
        scratch_shapes=[pltpu.VMEM((rows * comps, LANES), jnp.float32)],
    )(target, data, tables)


def on_device(records, fan_taps, dip_taps, live_mask, node_place, shot_place):
    _, comps, nodes, samples = records.shape
    taps = fan_taps.shape[1]
    reach = (taps - 1) // 2
    wide = 2 * reach
    devices = lax.axis_size("shot")
    group = nodes // devices

    block = records[0]
    low, high = time_halo(block, "tm", wide)
    live_col = samples + 32
    live = jnp.broadcast_to(live_mask[0].astype(jnp.bfloat16)[None, :, None], (comps, nodes, 1))
    gap1 = jnp.zeros((comps, nodes, live_col - samples - wide), jnp.bfloat16)
    gap2 = jnp.zeros((comps, nodes, EXT - wide - live_col - 1), jnp.bfloat16)
    ext = jnp.concatenate([block, high, gap1, live, gap2, low], axis=-1)
    place = lax.axis_index("tm")
    lane = jnp.arange(LANES, dtype=jnp.int32) % wide
    edge = jnp.where(lane < reach, place > 0, place < lax.axis_size("tm") - 1).astype(jnp.float32)[None, :]
    packed = fan_call(node_place[None, :], edge, ext, circulant(fan_taps, samples), live_col)

    data = lax.all_to_all(packed, "shot", split_axis=0, concat_axis=0, tiled=True)
    spread = comps * group
    target = (jnp.repeat(shot_place, group) * spread + jnp.tile(jnp.arange(group, dtype=jnp.int32), devices))[None, :]
    out = dip_call(target, data, circulant(dip_taps[None], samples), group, comps)
    return out.reshape(devices, comps, group, samples)


def solution(mesh):
    return jax.shard_map(
        on_device,
        mesh=mesh,
        in_specs=(P("shot", None, None, "tm"), P(), P(), P("shot", None), P(), P()),
        out_specs=P(None, None, "shot", "tm"),
        check_vma=False,
    )
```

```python
import functools

import jax
import jax.numpy as jnp
from jax import lax
from jax.experimental import pallas as pl
from jax.experimental.pallas import tpu as pltpu
from jax.sharding import PartitionSpec as P

LANES = 128
EXT = 256


def time_halo(block, axis, width):
    count = lax.axis_size(axis)
    forward = [(i, i + 1) for i in range(count - 1)]
    backward = [(target, source) for source, target in forward]
    samples = block.shape[-1]
    low = lax.ppermute(lax.slice_in_dim(block, samples - width, None, axis=-1), axis, forward)
    high = lax.ppermute(lax.slice_in_dim(block, 0, width, axis=-1), axis, backward)
    return low, high


def circulant(tap_set, samples):
    taps = tap_set.shape[-1]
    reach = (taps - 1) // 2
    j = jnp.arange(EXT, dtype=jnp.int32)
    t = jnp.arange(samples, dtype=jnp.int32)
    b = (j[:, None] - t[None, :] + reach) % EXT
    onehot = (b[:, :, None] == jnp.arange(taps, dtype=jnp.int32)[None, None, :]).astype(jnp.bfloat16)
    tables = jnp.einsum("gab,jtb->gajt", tap_set, onehot, preferred_element_type=jnp.float32)
    return tables.astype(jnp.bfloat16)


def fan_kernel(place_ref, edge_ref, ext_ref, table_ref, out_ref, scr_ref, halo_ref, *, taps, live_col, comps):
    step = pl.program_id(0)
    per = ext_ref.shape[0]
    rows = ext_ref.shape[1]
    samples = LANES
    reach = (taps - 1) // 2
    place = place_ref[...]
    select = (lax.broadcasted_iota(jnp.int32, (rows, rows), 0) == place).astype(jnp.bfloat16)
    lane = lax.broadcasted_iota(jnp.int32, (rows, LANES), 1)
    zeros = jnp.zeros((8, EXT), jnp.float32)
    scr_ref[0:8, :] = zeros
    scr_ref[rows + 8:rows + 16, :] = zeros
    keep = None
    for i in range(per):
        ordered = jnp.dot(select, ext_ref[i], preferred_element_type=jnp.float32)
        keep = ordered[:, live_col:live_col + 1]
        scr_ref[8:rows + 8, :] = ordered
        acc = jnp.zeros((rows, LANES), jnp.float32)
        acc_h = jnp.zeros((rows, LANES), jnp.float32)
        for a in range(taps):
            table = table_ref[i, a]
            both = jnp.concatenate([table, jnp.concatenate([table[samples:], table[:samples]], axis=0)], axis=1)
            moved = scr_ref[pl.ds(a + 8 - reach, rows), :].astype(jnp.bfloat16)
            part = jnp.dot(moved, both, preferred_element_type=jnp.float32)
            acc = acc + part[:, :samples]
            acc_h = acc_h + part[:, samples:]
        c = step * per + i
        out_ref[:, :, pl.ds(pl.multiple_of(c * samples, samples), samples)] = (acc * keep).astype(out_ref.dtype).reshape(rows // 2, 2, samples)
        for k in range(i, comps, per):
            @pl.when(c == k)
            def _():
                moved = pltpu.roll(acc_h, reach + 2 * reach * k, 1)
                mine = jnp.where((lane >= 2 * reach * k) & (lane < 2 * reach * (k + 1)), moved, 0.0)
                if k == 0:
                    halo_ref[...] = mine
                else:
                    halo_ref[...] += mine

    @pl.when(step == pl.num_programs(0) - 1)
    def _():
        out_ref[:, :, comps * samples:(comps + 1) * samples] = (halo_ref[...] * keep * edge_ref[...]).astype(out_ref.dtype).reshape(rows // 2, 2, samples)


def dip_kernel(target_ref, data_ref, table_ref, out_ref, *, taps, group, comps):
    rows = data_ref.shape[0] * data_ref.shape[1]
    samples = LANES
    reach = (taps - 1) // 2
    stride = comps * group
    out_rows = out_ref.shape[0]
    target = target_ref[...]
    row = lax.broadcasted_iota(jnp.int32, (out_rows, rows), 0)
    halo = data_ref[:, :, comps * samples:(comps + 1) * samples].reshape(rows, samples).astype(jnp.float32)
    selects, parts = [], []
    for c in range(comps):
        mine = pltpu.roll(halo, (samples - reach - 2 * reach * c) % samples, 1).astype(jnp.bfloat16)
        parts.append(jnp.concatenate([data_ref[:, :, c * samples:(c + 1) * samples].reshape(rows, samples), mine], axis=1))
        selects.append((row == target + group * c).astype(jnp.bfloat16))
    gathered = jnp.dot(jnp.concatenate(selects, axis=1), jnp.concatenate(parts, axis=0), preferred_element_type=jnp.float32)
    gathered = gathered.astype(jnp.bfloat16)
    acc = jnp.zeros((out_rows, LANES), jnp.float32)
    for first in range(0, taps, 2):
        pair = list(range(first, min(first + 2, taps)))
        tables = jnp.concatenate([table_ref[0, a] for a in pair], axis=1)
        both = jnp.dot(gathered, tables, preferred_element_type=jnp.float32)
        for k, a in enumerate(pair):
            part = both[:, k * samples:(k + 1) * samples]
            shift = stride * (a - reach)
            if shift > 0:
                part = jnp.concatenate([part[shift:], jnp.zeros((shift, LANES), jnp.float32)], axis=0)
            elif shift < 0:
                part = jnp.concatenate([jnp.zeros((-shift, LANES), jnp.float32), part[:shift]], axis=0)
            acc = acc + part
    out_ref[...] = acc.astype(out_ref.dtype)


def fan_call(place, edge, ext, tables, live_col):
    comps, rows, _ = ext.shape
    taps = tables.shape[1]
    kernel = functools.partial(fan_kernel, taps=taps, live_col=live_col, comps=comps)
    return pl.pallas_call(
        kernel,
        grid=(comps // 2,),
        in_specs=[
            pl.BlockSpec((1, rows), lambda c: (0, 0)),
            pl.BlockSpec((1, LANES), lambda c: (0, 0)),
            pl.BlockSpec((2, rows, EXT), lambda c: (c, 0, 0)),
            pl.BlockSpec((2, taps, EXT, LANES), lambda c: (c, 0, 0, 0)),
        ],
        out_specs=pl.BlockSpec((rows // 2, 2, (comps + 1) * LANES), lambda c: (0, 0, 0)),
        out_shape=jax.ShapeDtypeStruct((rows // 2, 2, (comps + 1) * LANES), jnp.bfloat16),
        scratch_shapes=[pltpu.VMEM((rows + 16, EXT), jnp.float32), pltpu.VMEM((rows, LANES), jnp.float32)],
    )(place, edge, ext, tables)


def dip_call(target, data, tables, group, comps):
    rows = data.shape[0] * data.shape[1]
    taps = tables.shape[1]
    kernel = functools.partial(dip_kernel, taps=taps, group=group, comps=comps)
    return pl.pallas_call(
        kernel,
        out_shape=jax.ShapeDtypeStruct((rows * comps, LANES), jnp.bfloat16),
    )(target, data, tables)


def on_device(records, fan_taps, dip_taps, live_mask, node_place, shot_place):
    _, comps, nodes, samples = records.shape
    taps = fan_taps.shape[1]
    reach = (taps - 1) // 2
    wide = 2 * reach
    devices = lax.axis_size("shot")
    group = nodes // devices

    block = records[0]
    low, high = time_halo(block, "tm", wide)
    live_col = samples + 32
    live = jnp.broadcast_to(live_mask[0].astype(jnp.bfloat16)[None, :, None], (comps, nodes, 1))
    gap1 = jnp.zeros((comps, nodes, live_col - samples - wide), jnp.bfloat16)
    gap2 = jnp.zeros((comps, nodes, EXT - wide - live_col - 1), jnp.bfloat16)
    ext = jnp.concatenate([block, high, gap1, live, gap2, low], axis=-1)
    place = lax.axis_index("tm")
    lane = jnp.arange(LANES, dtype=jnp.int32) % wide
    edge = jnp.where(lane < reach, place > 0, place < lax.axis_size("tm") - 1).astype(jnp.float32)[None, :]
    packed = fan_call(node_place[None, :], edge, ext, circulant(fan_taps, samples), live_col)

    data = lax.all_to_all(packed, "shot", split_axis=0, concat_axis=0, tiled=True)
    spread = comps * group
    target = (jnp.repeat(shot_place, group) * spread + jnp.tile(jnp.arange(group, dtype=jnp.int32), devices))[None, :]
    out = dip_call(target, data, circulant(dip_taps[None], samples), group, comps)
    return out.reshape(devices, comps, group, samples)


def solution(mesh):
    return jax.shard_map(
        on_device,
        mesh=mesh,
        in_specs=(P("shot", None, None, "tm"), P(), P(), P("shot", None), P(), P()),
        out_specs=P(None, None, "shot", "tm"),
        check_vma=False,
    )
```
